32 devices in a mesh: groups: 2 (over y), seq: 4 (over z), adapt: 4 (over x, core).
Axes of the slice: x: 2, y: 2, z: 4, core: 2. Of those that a mesh axis runs over, the one named last changes fastest.
Arguments:
- image: bfloat16 [16, 2048, 3072], P(('groups', 'adapt'), 'seq'), parts along dimension 0, may hold values from -6 to 6
- modulation: float32 [16, 2, 3072], P(('groups', 'adapt')), parts along dimension 0, may hold values from -3 to 3
- query_key_value_weight: bfloat16 [3072, 6144], P(None, 'adapt'), may hold values from -0.109375 to 0.109375
- pooled_down_factor: bfloat16 [16, 3072, 64], P('seq'), may hold values from -0.109375 to 0.109375
- pooled_up_factor: bfloat16 [16, 64, 6144], P('seq', None, 'adapt'), may hold values from -0.75 to 0.75
- request_adapter: int32 [16], P('groups'), parts along dimension 0, may hold values from 0 to 15
- adapter_slot_table: int32 [16], replicated, may hold values from 0 to 15, each once
- row_request: int32 [16], P('groups'), parts along dimension 0, may hold values from 0 to 7, each once
- text_key_value: bfloat16 [16, 512, 2, 2048], P('groups', 'seq', None, 'adapt'), parts along dimension 0, may hold values from -110 to 110
- query_key_gain: float32 [2, 128], replicated, may hold values from 1 to 2.5
Outputs:
- attended: bfloat16 [16, 2048, 2048], P('groups', 'seq', 'adapt'), parts along dimension 0
The draws below stay inside these ranges and needn't reach their ends.
There are 2 independent parts, one for each index of `groups`. The reference program is written for one: setup_inputs(seed, part) draws one part's arguments, and reference() takes and returns one part's arrays. A program takes and returns all parts, laid end to end along the dimension named above; an argument that names none is the same for every part. Nothing has to cross between parts.
All inputs are finite; a program needn't handle non-finite values.
Results may differ from the reference program's by a relative error of at most 0.0049.
The reference program's roundings to bfloat16 on the way (of `modulated`, `shrunk` and `probs`) count: a program that leaves them out, or rounds other values in their place, can miss the bound.
Values may be sent and summed in bfloat16 or wider, within the bound.
A program may use at most 192 MiB of HBM per device.

```python
import math
import jax
import jax.numpy as jnp
import numpy as np
from jax import lax

MODEL_WIDTH = 3072
HEAD_SIZE = 128
LOCAL_HEADS = 16
ADAPTER_RANK = 64
IMG = 2048
TXT = 512
REQS = 8
ADAPTER_POOL = 16


def draw_text_key_value(key, part):
    first = jax.random.fold_in(key, 0)
    array_shape = (REQS, TXT, 2, LOCAL_HEADS * HEAD_SIZE)
    return jnp.clip(jax.random.normal(first, array_shape, jnp.float32), -6.0, 6.0).astype(jnp.bfloat16)


def place_ends(drawn, key, low, high):
    dims = drawn.shape
    index_at = [jax.random.randint(jax.random.fold_in(key, axis), (), 0, dims[axis]) for axis in range(len(dims))]
    drawn = drawn.at[tuple(index_at)].set(low)
    longest = dims.index(max(dims))
    index_at[longest] = (index_at[longest] + 1) % dims[longest]
    return drawn.at[tuple(index_at)].set(high)


def level_of(key, extent, cuts, least, high):
    loudness, own = 1.0, jax.random.fold_in(key, 6)
    for axis_at, blocks in cuts:
        draws = jnp.exp(jax.random.uniform(jax.random.fold_in(own, axis_at), (blocks,), jnp.float32, least / len(cuts), high / len(cuts)))
        loudness = loudness * jnp.repeat(draws, extent[axis_at] // blocks).reshape([-1 if axis == axis_at else 1 for axis in range(len(extent))])
    return loudness


def rank_table(amount, lean):
    weights = [(1 << 20) // math.isqrt(grade ** lean) + 1 for grade in range(1, amount + 1)]
    width = 1 + sum(weights) // (1 << 30)
    return np.cumsum(np.array([max(1, weight // width) for weight in weights]))


def ranked(stream_key, extent, count, slope):
    listing = rank_table(count, slope)
    ticket = jax.random.randint(jax.random.fold_in(stream_key, 1), extent, 0, int(listing[count - 1]))
    grade = jnp.searchsorted(jnp.asarray(listing, jnp.int32), ticket, side="right")
    return jax.random.permutation(jax.random.fold_in(stream_key, 2), count)[grade].astype(jnp.int32)


def scatter_about(key, dims, spread, most, cuts=(), held_as=jnp.bfloat16):
    values = jax.random.normal(key, dims, jnp.float32) * spread
    if len(cuts) > 0:
        values = level_of(key, dims, cuts, -0.22, 0.18) * values
    return jnp.clip(values, min=-most, max=most).astype(held_as)


def setup_inputs(seed: int = 0, part: int = 0) -> dict:
    streams_of = jax.random.split(jax.random.key(seed), 11)
    part_keys = jax.random.split(jax.random.fold_in(streams_of[10], part), 11)
    image = scatter_about(part_keys[0], (REQS, IMG, MODEL_WIDTH), 1.0, 6.0, ((0, 4), (1, 4)))
    modulation = scatter_about(part_keys[1], (REQS, 2, MODEL_WIDTH), 0.5, 3.0, ((0, 4),), jnp.float32)
    query_key_value_weight = scatter_about(streams_of[2], (MODEL_WIDTH, 3 * LOCAL_HEADS * HEAD_SIZE), MODEL_WIDTH ** -0.5, 0.109375, ((1, 4),))
    pooled_down_factor = scatter_about(streams_of[3], (ADAPTER_POOL, MODEL_WIDTH, ADAPTER_RANK), MODEL_WIDTH ** -0.5, 0.109375, ((0, 4),))
    pooled_up_factor = scatter_about(streams_of[4], (ADAPTER_POOL, ADAPTER_RANK, 3 * LOCAL_HEADS * HEAD_SIZE), ADAPTER_RANK ** -0.5, 0.75, ((0, 4), (2, 4)))
    request_adapter = place_ends(ranked(part_keys[5], (REQS,), ADAPTER_POOL, 2), jax.random.fold_in(part_keys[5], 3), 0, ADAPTER_POOL - 1).astype(jnp.int32)
    adapter_slot_table = jax.random.permutation(streams_of[6], ADAPTER_POOL).astype(jnp.int32)
    row_request = jax.random.permutation(part_keys[7], REQS).astype(jnp.int32)
    text_key_value = draw_text_key_value(jax.random.fold_in(jax.random.fold_in(streams_of[10], part), 71), part)
    query_key_gain = jnp.clip(jnp.exp(jax.random.uniform(streams_of[9], (2, HEAD_SIZE), jnp.float32, math.log(1.0), math.log(2.5))), 1.0, 2.5)
    return {"image": image, "modulation": modulation, "query_key_value_weight": query_key_value_weight, "pooled_down_factor": pooled_down_factor, "pooled_up_factor": pooled_up_factor, "request_adapter": request_adapter, "adapter_slot_table": adapter_slot_table, "row_request": row_request, "text_key_value": text_key_value, "query_key_gain": query_key_gain}


def rms_scale(values, gain):
    return values * lax.rsqrt(lax.optimization_barrier(jnp.mean(values * values, axis=-1, keepdims=True)) + 1e-06) * gain

def reference(image, modulation, query_key_value_weight, pooled_down_factor, pooled_up_factor, request_adapter, adapter_slot_table, row_request, text_key_value, query_key_gain):
    widened = image.astype(jnp.float32)
    centre = widened - lax.optimization_barrier(jnp.mean(widened, axis=-1, keepdims=True))
    variance = lax.optimization_barrier(jnp.mean(centre * centre, axis=-1, keepdims=True))
    normed = centre * lax.rsqrt(variance + 1e-06)
    modulated = ((1.0 + modulation[:, 1, None, :]) * normed + modulation[:, 0, None, :]).astype(jnp.bfloat16)
    slots = adapter_slot_table[request_adapter[row_request]].astype(jnp.int32)
    inverse = 1.0 / HEAD_SIZE ** 0.5

    def per_head(operands):
        head_q, head_k, head_v = operands
        scores = jnp.einsum('qd,kd->qk', head_q.astype(jnp.float32), head_k.astype(jnp.float32)) * inverse
        probs = jax.nn.softmax(scores, axis=-1).astype(jnp.bfloat16)
        return jnp.dot(probs, head_v, preferred_element_type=jnp.float32).astype(jnp.bfloat16)

    def per_request(operands):
        token_rows, storage_slot, text_part = operands
        down_factor = pooled_down_factor[storage_slot]
        up_factor = pooled_up_factor[storage_slot]
        shrunk = jnp.dot(token_rows, down_factor, preferred_element_type=jnp.float32).astype(jnp.bfloat16)
        qkv = jnp.dot(token_rows, query_key_value_weight, preferred_element_type=jnp.float32)
        qkv = qkv + jnp.dot(shrunk, up_factor, preferred_element_type=jnp.float32)
        qkv = qkv.reshape(IMG, LOCAL_HEADS, 3, HEAD_SIZE)
        queries = rms_scale(qkv[:, :, 0], query_key_gain[0]).astype(jnp.bfloat16)
        image_keys = rms_scale(qkv[:, :, 1], query_key_gain[1]).astype(jnp.bfloat16)
        image_values = qkv[:, :, 2].astype(jnp.bfloat16)
        text_keys = text_part[:, 0].reshape(TXT, LOCAL_HEADS, HEAD_SIZE)
        text_values = text_part[:, 1].reshape(TXT, LOCAL_HEADS, HEAD_SIZE)
        all_keys = jnp.concatenate([image_keys, text_keys], axis=0)
        all_values = jnp.concatenate([image_values, text_values], axis=0)
        outputs = lax.map(per_head, (jnp.transpose(queries, (1, 0, 2)), jnp.transpose(all_keys, (1, 0, 2)), jnp.transpose(all_values, (1, 0, 2))))
        return jnp.transpose(outputs, (1, 0, 2)).reshape(IMG, LOCAL_HEADS * HEAD_SIZE)
    return lax.map(per_request, (modulated, slots, text_key_value))
```

```python
import functools
import math

import jax
import jax.numpy as jnp
from jax import lax
from jax.experimental import pallas as pl
from jax.experimental.pallas import tpu as pltpu
from jax.sharding import PartitionSpec as P

HEAD_SIZE = 128


def layer_modulate(image, modulation):
    widened = image.astype(jnp.float32)
    centre = widened - jnp.mean(widened, axis=-1, keepdims=True)
    variance = jnp.mean(centre * centre, axis=-1, keepdims=True)
    normed = centre * lax.rsqrt(variance + 1e-06)
    return ((1.0 + modulation[:, 1, None, :]) * normed + modulation[:, 0, None, :]).astype(
        jnp.bfloat16
    )


def rms_scale(values, gain):
    return values * lax.rsqrt(jnp.mean(values * values, axis=-1, keepdims=True) + 1e-06) * gain


def attend_item(operands):
    queries, joined = operands
    key_rows = joined[:, 0]
    value_rows = joined[:, 1]
    query_count = queries.shape[0]
    block = math.gcd(query_count, 512)
    inverse = 1.0 / math.sqrt(queries.shape[-1])
    blocked = queries.reshape(query_count // block, block, queries.shape[-1])

    def one_block(block_rows):
        scores = (
            lax.dot_general(
                block_rows, key_rows, (((1,), (1,)), ((), ())), preferred_element_type=jnp.float32
            )
            * inverse
        )
        highest = jnp.max(scores, axis=-1, keepdims=True)
        weights = jnp.exp(scores - highest)
        weights = weights / jnp.sum(weights, axis=-1, keepdims=True)
        return jnp.dot(
            weights.astype(jnp.bfloat16), value_rows, preferred_element_type=jnp.float32
        ).astype(jnp.bfloat16)

    return lax.map(one_block, blocked).reshape(queries.shape)


def general_device(
    image,
    modulation,
    query_key_value_weight,
    pooled_down_factor,
    pooled_up_factor,
    request_adapter,
    adapter_slot_table,
    row_request,
    text_key_value,
    query_key_gain,
):
    seq_index = lax.axis_index("seq")
    all_requests = request_adapter.shape[0]
    local_pool_slice = pooled_down_factor.shape[0]
    pool_total = adapter_slot_table.shape[0]
    heads_local = query_key_value_weight.shape[1] // (3 * HEAD_SIZE)
    text_local = text_key_value.shape[1]
    modulated = layer_modulate(image, modulation)
    request_match = row_request[:, None] == jnp.arange(all_requests, dtype=jnp.int32)[None, :]
    chosen_ids = jnp.sum(jnp.where(request_match, request_adapter[None, :], 0), axis=1)
    slot_match = chosen_ids[:, None] == jnp.arange(pool_total, dtype=jnp.int32)[None, :]
    slots = jnp.sum(jnp.where(slot_match, adapter_slot_table[None, :], 0), axis=1)
    owned = slots // local_pool_slice == seq_index
    local_match = (slots % local_pool_slice)[:, None] == jnp.arange(
        local_pool_slice, dtype=jnp.int32
    )[None, :]
    slot_picker = (owned[:, None] & local_match).astype(jnp.bfloat16)
    up_terms = jnp.einsum(
        "eq,qfx->efx", slot_picker, pooled_up_factor, preferred_element_type=jnp.float32
    ).astype(jnp.bfloat16)
    down_terms = jnp.einsum(
        "mv,vna->mna", slot_picker, pooled_down_factor, preferred_element_type=jnp.float32
    ).astype(jnp.bfloat16)
    down_fetched, up_fetched = (
        lax.psum(down_terms, "seq").astype(jnp.float32),
        lax.psum(up_terms, "seq").astype(jnp.float32),
    )
    down_fetched = down_fetched.astype(jnp.bfloat16)
    up_fetched = up_fetched.astype(jnp.bfloat16)
    block_rows = lax.all_gather(modulated, "adapt", axis=0, tiled=True)
    shrunk = jnp.einsum(
        "rtd,rdk->rtk", block_rows, down_fetched, preferred_element_type=jnp.float32
    ).astype(jnp.bfloat16)
    frozen = jnp.einsum(
        "rtd,dc->rtc", block_rows, query_key_value_weight, preferred_element_type=jnp.float32
    )
    qkv = frozen + jnp.einsum(
        "rtk,rkc->rtc", shrunk, up_fetched, preferred_element_type=jnp.float32
    )
    token_local = qkv.shape[1]
    qkv = qkv.reshape(all_requests, token_local, heads_local, 3, HEAD_SIZE)
    queries = rms_scale(qkv[:, :, :, 0], query_key_gain[0]).astype(jnp.bfloat16)
    image_keys = rms_scale(qkv[:, :, :, 1], query_key_gain[1]).astype(jnp.bfloat16)
    image_values = qkv[:, :, :, 2].astype(jnp.bfloat16)
    image_pairs = jnp.transpose(jnp.stack([image_keys, image_values], axis=3), (0, 2, 1, 3, 4))
    text_pairs = jnp.transpose(
        text_key_value.reshape(all_requests, text_local, 2, heads_local, HEAD_SIZE), (0, 3, 1, 2, 4)
    )
    joined = jnp.concatenate([image_pairs, text_pairs], axis=2)
    joined = joined.reshape(all_requests * heads_local, token_local + text_local, 2, HEAD_SIZE)
    queries = jnp.transpose(queries, (0, 2, 1, 3)).reshape(
        all_requests * heads_local, token_local, HEAD_SIZE
    )
    query_items, joined_items = (
        lax.all_to_all(queries, "seq", split_axis=0, concat_axis=1, tiled=True),
        lax.all_to_all(joined, "seq", split_axis=0, concat_axis=1, tiled=True),
    )
    attended = lax.map(attend_item, (query_items, joined_items))
    returned = lax.all_to_all(attended, "seq", split_axis=1, concat_axis=0, tiled=True)
    returned = returned.reshape(all_requests, heads_local, token_local, HEAD_SIZE)
    return jnp.transpose(returned, (0, 2, 1, 3)).reshape(
        all_requests, token_local, heads_local * HEAD_SIZE
    )


BF16 = jnp.bfloat16
ROUNDS = 8
EARLY = 2
F32 = jnp.float32
ANY = pl.BlockSpec(memory_space=pl.ANY)
WHOLE = pl.BlockSpec(memory_space=pltpu.VMEM)


def flipped(index, k):
    low = 1 - 2 * lax.rem(index, 2) if k % 2 else 0
    high = 2 - 4 * (index // 2) if k // 2 else 0
    return index + low + high


def block_kernel(
    image, modulation, weight, down, up, gain, text,
    out, tok,
    weight_held, mod, rows_held, q_held, k_held, v_held, txt,
    up_near, down_near, up_sent, down_sent, up_far, down_far, down_all, down_whole,
    image_sem, weight_sem, load_sem,
    tok_send, tok_recv, side_send, side_recv, across_send, across_recv, last_send, last_recv,
    near_send, near_recv, far_send, far_recv, spread_send, spread_recv,
    text_send, text_recv, out_send, out_recv,
):
    s = lax.axis_index("seq")
    a = lax.axis_index("adapt")
    x = a // 2
    c = lax.rem(a, 2)
    me = s * 4 + a
    sibling = {"seq": s, "adapt": 2 * x + 1 - c}
    partner = {"seq": s, "adapt": 2 * (1 - x) + c}
    request_row = (x, 1 - x)
    piece_rows = tok.shape[4]
    width = tok.shape[5]
    chunk_rows = 8 * piece_rows
    head_columns = q_held.shape[5]
    heads = head_columns // HEAD_SIZE
    token_local = 2 * ROUNDS * piece_rows
    half_rows = ROUNDS * piece_rows
    text_rows = 4 * txt.shape[2]

    def remote(source, target, send, recv, device):
        return pltpu.make_async_remote_copy(
            src_ref=source, dst_ref=target, send_sem=send, recv_sem=recv,
            device_id=device, device_id_type=pl.DeviceIdType.MESH,
        )

    weight_copy = pltpu.make_async_copy(weight, weight_held, weight_sem)

    def image_copy(n):
        return pltpu.make_async_copy(image.at[:, :, n], mod.at[:, :, n], image_sem.at[n])

    for n in range(ROUNDS):
        image_copy(n).start()
    weight_copy.start()

    barrier = pltpu.get_barrier_semaphore()
    for k in range(1, 16):
        other = lax.rem(me + k, 16)
        pl.semaphore_signal(
            barrier, inc=1, device_id={"seq": other // 4, "adapt": lax.rem(other, 4)},
            device_id_type=pl.DeviceIdType.MESH,
        )
    pl.semaphore_wait(barrier, 15)

    def near_copies():
        to = {"seq": flipped(s, 1), "adapt": a}
        copies = []
        for n, k in enumerate((1, 3)):
            place = flipped(s, k)
            copies.append(remote(up.at[:, place], up_near.at[n], near_send.at[n], near_recv.at[n], to))
            copies.append(
                remote(down.at[:, place], down_near.at[n], near_send.at[2 + n], near_recv.at[2 + n], to)
            )
        return copies

    def far_copies():
        to = {"seq": flipped(s, 2), "adapt": a}
        return [
            remote(up_sent, up_far, far_send.at[0], far_recv.at[0], to),
            remote(down_sent, down_far, far_send.at[1], far_recv.at[1], to),
        ]

    def spread_copy(k):
        return remote(
            down_all.at[a], down_all.at[a], spread_send.at[k], spread_recv.at[k],
            {"seq": s, "adapt": flipped(a, k)},
        )

    def spread_in(k):
        other = flipped(a, k)
        return remote(
            down_all.at[other], down_all.at[other], spread_send.at[k], spread_recv.at[k], sibling
        )

    for copy in near_copies():
        copy.start()

    def handed(n, j, h):
        place = 2 * c + j
        mine = jnp.logical_and(place == s, c == h)
        recv = tok_recv.at[n, s]
        source, target = mod.at[j, h, n], tok.at[0, s, h, n]
        away = remote(
            source, target, tok_send.at[n, 2 * j + h], recv, {"seq": place, "adapt": 2 * x + h}
        )
        return mine, away, pltpu.make_async_copy(source, target, recv)

    def start_round(n):
        for j in range(2):
            for h in range(2):
                mine, away, here = handed(n, j, h)

                @pl.when(mine)
                def _():
                    here.start()

                @pl.when(jnp.logical_not(mine))
                def _():
                    away.start()

    def end_round(n):
        for j in range(2):
            for h in range(2):
                mine, away, _ = handed(n, j, h)

                @pl.when(jnp.logical_not(mine))
                def _():
                    away.wait_send()

    def modulate_round(n):
        image_copy(n).wait()
        step_rows = 16
        parts = piece_rows // step_rows

        def one(b, carry):
            j = b // (2 * parts)
            h = lax.rem(b // parts, 2)
            rows = pl.ds(pl.multiple_of(lax.rem(b, parts) * step_rows, step_rows), step_rows)
            widened = mod[j, h, n, rows, :].astype(F32)
            centre = widened - jnp.mean(widened, axis=-1, keepdims=True)
            variance = jnp.mean(centre * centre, axis=-1, keepdims=True)
            normed = centre * lax.rsqrt(variance + 1e-06)
            shift = modulation[j, 0:1, :]
            scale = modulation[j, 1:2, :]
            mod[j, h, n, rows, :] = ((1.0 + scale) * normed + shift).astype(BF16)
            return carry

        lax.fori_loop(0, 4 * parts, one, 0)

    def piece(i, n, k, core):
        return tok.at[i, flipped(s, k), core, n]

    def first(n, k):
        here = piece(0, n, k, c)
        return remote(here, here, tok_send.at[n, 0], tok_recv.at[n, flipped(s, k)], sibling)

    def side(n, k):
        here = piece(0, n, k, c)
        return remote(here, here, side_send.at[n, k], side_recv.at[n, k], sibling)

    def side_in(n, k):
        there = piece(0, n, k, 1 - c)
        return remote(there, there, side_send.at[n, k], side_recv.at[n, k], sibling)

    def across(n, k):
        return remote(
            piece(0, n, k, c), piece(1, n, k, c), across_send.at[n, k], across_recv.at[n, k], partner
        )

    def last(n, k):
        here = piece(1, n, k, c)
        return remote(here, here, last_send.at[n, k], last_recv.at[n, k], sibling)

    def last_in(n, k):
        there = piece(1, n, k, 1 - c)
        return remote(there, there, last_send.at[n, k], last_recv.at[n, k], sibling)

    def text_copy(i, k):
        place = flipped(s, k)
        row = request_row[i]
        return remote(
            text.at[row, place], txt.at[i, s], text_send.at[i, k], text_recv.at[i, k],
            {"seq": place, "adapt": a},
        )

    def text_in(i, k):
        place = flipped(s, k)
        return remote(
            txt.at[i, place], txt.at[i, place], text_send.at[i, k], text_recv.at[i, k], sibling
        )

    def own_text(i):
        return pltpu.make_async_copy(text.at[request_row[i], s], txt.at[i, s], text_recv.at[i, 0])

    for i in range(2):
        own_text(i).start()

    def opening(n, carry):
        modulate_round(n)

        @pl.when(n < EARLY)
        def _():
            start_round(n)

        return carry

    lax.fori_loop(0, ROUNDS, opening, 0)

    for copy in near_copies():
        copy.wait_recv()
    away = flipped(s, 2)
    up_sent[...] = up[:, away] + up_near[1]
    down_sent[...] = down[:, away] + down_near[1]
    for copy in far_copies():
        copy.start()
    up_near[0] = up[:, s] + up_near[0]
    down_near[0] = down[:, s] + down_near[0]

    def start_rest(n, carry):
        start_round(n)
        return carry

    lax.fori_loop(EARLY, ROUNDS, start_rest, 0)
    for i in range(2):
        for k in (2, 3, 1):
            text_copy(i, k).start()

    def pass_on(n):
        for k in range(4):
            first(n, k).wait_recv()
            across(n, k).start()
            side(n, k).start()

    def load(i, n):
        return pltpu.make_async_copy(tok.at[i, :, :, n], rows_held.at[i], load_sem.at[i])

    def project(i, n):
        rows = rows_held[i].reshape(chunk_rows, width)
        row = request_row[i]
        shrunk = lax.dot_general(
            rows, down_whole[row], (((1,), (1,)), ((), ())), preferred_element_type=F32
        ).astype(BF16)
        wide = 6 * HEAD_SIZE
        for part in range(weight_held.shape[1] // wide):
            columns = slice(part * wide, (part + 1) * wide)
            qkv = jnp.dot(rows, weight_held[:, columns], preferred_element_type=F32)
            qkv = qkv + jnp.dot(shrunk, up_far[row, :, columns], preferred_element_type=F32)
            for h in range(2):
                head = slice((2 * part + h) * HEAD_SIZE, (2 * part + h + 1) * HEAD_SIZE)
                q, k, v = (
                    qkv[:, (3 * h + m) * HEAD_SIZE : (3 * h + m + 1) * HEAD_SIZE] for m in range(3)
                )
                shape = (4, 2, piece_rows, HEAD_SIZE)
                q_held[i, :, :, n, :, head] = rms_scale(q, gain[0:1, :]).astype(BF16).reshape(shape)
                k_held[i, :, :, n, :, head] = rms_scale(k, gain[1:2, :]).astype(BF16).reshape(shape)
                v_held[i, :, :, n, :, head] = v.astype(BF16).reshape(shape)

    pass_on(0)
    pass_on(1)
    for copy in far_copies():
        copy.wait_recv()
    up_far[...] = up_near[0] + up_far[...]
    down_all[a] = down_near[0] + down_far[...]
    for k in range(1, 4):
        spread_copy(k).start()
    weight_copy.wait()

    def stage(n, carry):
        @pl.when(n < ROUNDS)
        def _():
            pass_on(n)

        @pl.when(n == 2)
        def _():
            for k in range(1, 4):
                spread_in(k).wait_recv()
            share = down_all.shape[3]
            for k in range(4):
                down_whole[:, :, k * share : (k + 1) * share] = down_all[k]

        @pl.when(n < ROUNDS + 2)
        def _():
            for k in range(4):
                side_in(n - 2, k).wait_recv()
            load(0, n - 2).start()
            for k in range(4):
                across(n - 2, k).wait_recv()
                last(n - 2, k).start()

        @pl.when(n > 2)
        def _():
            for k in range(4):
                last_in(n - 3, k).wait_recv()
            load(1, n - 3).start()

        @pl.when(n < ROUNDS + 2)
        def _():
            load(0, n - 2).wait()
            project(0, n - 2)

        @pl.when(n > 2)
        def _():
            load(1, n - 3).wait()
            project(1, n - 3)

        return carry

    lax.fori_loop(2, ROUNDS + 3, stage, 0)

    factor = math.log2(math.e) / math.sqrt(HEAD_SIZE)

    def target(step):
        return jnp.where(
            step == 3, s,
            jnp.where(step == 2, flipped(s, 1), jnp.where(step == 1, flipped(s, 3), flipped(s, 2))),
        )

    def out_copy(i, part, slot, row_from, place):
        row = 4 * jnp.where(i == 0, x, 1 - x) + row_from
        return remote(
            q_held.at[i, place, part], out.at[row, part], out_send.at[slot], out_recv.at[slot],
            {"seq": place, "adapt": a},
        )

    def own_out(i, part, slot):
        row = 4 * jnp.where(i == 0, x, 1 - x) + s
        return pltpu.make_async_copy(q_held.at[i, s, part], out.at[row, part], out_recv.at[slot])

    def attend_step(slot, carry):
        i = slot // 8
        step = lax.rem(slot // 2, 4)
        part = lax.rem(slot, 2)
        place = target(step)

        for r in range(2):
            @pl.when(slot == 8 * r)
            def _():
                own_text(r).wait()
                for k in range(1, 4):
                    text_in(r, k).wait_recv()

        def scores(h):
            head = slice(h * HEAD_SIZE, (h + 1) * HEAD_SIZE)
            query = q_held[i, place, part, :, :, head].reshape(half_rows, HEAD_SIZE)
            image_keys = k_held[i, :, :, :, :, head].reshape(4 * token_local, HEAD_SIZE)
            text_keys = txt[i, :, :, head].reshape(text_rows, HEAD_SIZE)
            return tuple(
                lax.dot_general(
                    query, key_rows, (((1,), (1,)), ((), ())), preferred_element_type=F32
                )
                for key_rows in (image_keys, text_keys)
            )

        ready = scores(0)
        for h in range(heads):
            one, two = ready
            if h + 1 < heads:
                ready = scores(h + 1)
            head = slice(h * HEAD_SIZE, (h + 1) * HEAD_SIZE)
            value_head = slice(head_columns + h * HEAD_SIZE, head_columns + (h + 1) * HEAD_SIZE)
            highest = jnp.maximum(
                jnp.max(one, axis=-1, keepdims=True), jnp.max(two, axis=-1, keepdims=True)
            )
            one = jnp.exp2((one - highest) * factor)
            two = jnp.exp2((two - highest) * factor)
            share = 1.0 / (jnp.sum(one, axis=-1, keepdims=True) + jnp.sum(two, axis=-1, keepdims=True))
            image_values = v_held[i, :, :, :, :, head].reshape(4 * token_local, HEAD_SIZE)
            text_values = txt[i, :, :, value_head].reshape(text_rows, HEAD_SIZE)
            total = jnp.dot((one * share).astype(BF16), image_values, preferred_element_type=F32)
            total = total + jnp.dot(
                (two * share).astype(BF16), text_values, preferred_element_type=F32
            )
            q_held[i, place, part, :, :, head] = total.astype(BF16).reshape(
                ROUNDS, piece_rows, HEAD_SIZE
            )

        @pl.when(step == 3)
        def _():
            own_out(i, part, slot).start()

        @pl.when(step < 3)
        def _():
            out_copy(i, part, slot, s, place).start()

        return carry

    lax.fori_loop(0, 16, attend_step, 0)

    def finish_round(n, carry):
        end_round(n)
        for k in range(4):
            side(n, k).wait_send()
            across(n, k).wait_send()
            last(n, k).wait_send()
        return carry

    lax.fori_loop(0, ROUNDS, finish_round, 0)
    for copy in near_copies() + far_copies():
        copy.wait_send()
    for k in range(1, 4):
        spread_copy(k).wait_send()
        for i in range(2):
            text_copy(i, k).wait_send()

    def finish_out(slot, carry):
        i = slot // 8
        step = lax.rem(slot // 2, 4)
        part = lax.rem(slot, 2)
        place = target(step)

        @pl.when(step == 3)
        def _():
            own_out(i, part, slot).wait()

        @pl.when(step < 3)
        def _():
            out_copy(i, part, slot, place, place).wait()

        return carry

    lax.fori_loop(0, 16, finish_out, 0)


def on_device(
    image,
    modulation,
    query_key_value_weight,
    pooled_down_factor,
    pooled_up_factor,
    request_adapter,
    adapter_slot_table,
    row_request,
    text_key_value,
    query_key_gain,
):
    seq_index = lax.axis_index("seq")
    all_requests = request_adapter.shape[0]
    pool_local, width, rank = pooled_down_factor.shape
    pool_total = adapter_slot_table.shape[0]
    columns = query_key_value_weight.shape[1]
    head_columns = columns // 3
    text_local = text_key_value.shape[1]
    token_local = image.shape[1]
    request_match = row_request[:, None] == jnp.arange(all_requests, dtype=jnp.int32)[None, :]
    chosen_ids = jnp.sum(jnp.where(request_match, request_adapter[None, :], 0), axis=1)
    slot_match = chosen_ids[:, None] == jnp.arange(pool_total, dtype=jnp.int32)[None, :]
    slots = jnp.sum(jnp.where(slot_match, adapter_slot_table[None, :], 0), axis=1)
    owned = slots // pool_local == seq_index
    local_match = (slots % pool_local)[:, None] == jnp.arange(pool_local, dtype=jnp.int32)[None, :]
    slot_picker = (owned[:, None] & local_match).astype(BF16)
    share = width // 4
    down_part = lax.dynamic_slice_in_dim(
        pooled_down_factor, lax.axis_index("adapt") * share, share, axis=1
    )
    down_terms = jnp.einsum(
        "mv,vna->man", slot_picker, down_part, preferred_element_type=F32
    ).astype(BF16)
    up_terms = jnp.einsum(
        "eq,qfx->efx", slot_picker, pooled_up_factor, preferred_element_type=F32
    ).astype(BF16)

    piece_rows = token_local // (2 * ROUNDS)
    held = pltpu.VMEM((2, 4, 2, ROUNDS, piece_rows, head_columns), BF16)

    def dma(*shape):
        return pltpu.SemaphoreType.DMA(shape)

    out, _ = pl.pallas_call(
        block_kernel,
        out_shape=(
            jax.ShapeDtypeStruct((all_requests, 2, ROUNDS, piece_rows, head_columns), BF16),
            jax.ShapeDtypeStruct((2, 4, 2, ROUNDS, piece_rows, width), BF16),
        ),
        in_specs=[ANY, WHOLE, ANY, WHOLE, WHOLE, WHOLE, ANY],
        out_specs=(ANY, ANY),
        scratch_shapes=[
            pltpu.VMEM((width, columns), BF16),
            pltpu.VMEM((2, 2, ROUNDS, piece_rows, width), BF16),
            pltpu.VMEM((2, 4, 2, piece_rows, width), BF16),
            held, held, held,
            pltpu.VMEM((2, 4, text_local, 2 * head_columns), BF16),
            pltpu.VMEM((2, 2, rank, columns), BF16),
            pltpu.VMEM((2, 2, rank, share), BF16),
            pltpu.VMEM((2, rank, columns), BF16),
            pltpu.VMEM((2, rank, share), BF16),
            pltpu.VMEM((2, rank, columns), BF16),
            pltpu.VMEM((2, rank, share), BF16),
            pltpu.VMEM((4, 2, rank, share), BF16),
            pltpu.VMEM((2, rank, width), BF16),
            dma(ROUNDS), dma(), dma(2),
        ]
        + [dma(ROUNDS, 4)] * 8
        + [dma(4)] * 2 + [dma(2)] * 2 + [dma(4)] * 2
        + [dma(2, 4)] * 2 + [dma(16)] * 2,
        compiler_params=pltpu.CompilerParams(
            collective_id=0, has_side_effects=True, vmem_limit_bytes=58 * 2**20
        ),
        name="block",
    )(
        image.reshape(2, 2, ROUNDS, piece_rows, width),
        modulation,
        query_key_value_weight,
        down_terms.reshape(2, 4, rank, share),
        up_terms.reshape(2, 4, rank, columns),
        query_key_gain,
        text_key_value.reshape(2, 4, text_local, 2 * head_columns),
    )
    return out.reshape(all_requests, token_local, head_columns)


def solution(mesh):
    in_specs = (
        P(("groups", "adapt"), "seq", None),
        P(("groups", "adapt"), None, None),
        P(None, "adapt"),
        P("seq", None, None),
        P("seq", None, "adapt"),
        P("groups"),
        P(),
        P("groups"),
        P("groups", "seq", None, "adapt"),
        P(),
    )
    out_specs = P("groups", "seq", "adapt")
    def chosen(*operands):
        image, request_adapter = operands[0], operands[5]
        fits = (
            mesh.shape["seq"] == 4
            and mesh.shape["adapt"] == 4
            and request_adapter.shape[0] == 8
            and image.shape[0] == 2
            and operands[2].shape[1] % (6 * HEAD_SIZE) == 0
            and image.shape[1] % 256 == 0
            and image.shape[2] % 512 == 0
        )
        return (on_device if fits else general_device)(*operands)

    return jax.shard_map(
        chosen, mesh=mesh, in_specs=in_specs, out_specs=out_specs, check_vma=False
    )
```

```python
import functools
import math

import jax
import jax.numpy as jnp
from jax import lax
from jax.experimental import pallas as pl
from jax.experimental.pallas import tpu as pltpu
from jax.sharding import PartitionSpec as P

HEAD_SIZE = 128


def layer_modulate(image, modulation):
    widened = image.astype(jnp.float32)
    centre = widened - jnp.mean(widened, axis=-1, keepdims=True)
    variance = jnp.mean(centre * centre, axis=-1, keepdims=True)
    normed = centre * lax.rsqrt(variance + 1e-06)
    return ((1.0 + modulation[:, 1, None, :]) * normed + modulation[:, 0, None, :]).astype(
        jnp.bfloat16
    )


def rms_scale(values, gain):
    return values * lax.rsqrt(jnp.mean(values * values, axis=-1, keepdims=True) + 1e-06) * gain


def attend_item(operands):
    queries, joined = operands
    key_rows = joined[:, 0]
    value_rows = joined[:, 1]
    query_count = queries.shape[0]
    block = math.gcd(query_count, 512)
    inverse = 1.0 / math.sqrt(queries.shape[-1])
    blocked = queries.reshape(query_count // block, block, queries.shape[-1])

    def one_block(block_rows):
        scores = (
            lax.dot_general(
                block_rows, key_rows, (((1,), (1,)), ((), ())), preferred_element_type=jnp.float32
            )
            * inverse
        )
        highest = jnp.max(scores, axis=-1, keepdims=True)
        weights = jnp.exp(scores - highest)
        weights = weights / jnp.sum(weights, axis=-1, keepdims=True)
        return jnp.dot(
            weights.astype(jnp.bfloat16), value_rows, preferred_element_type=jnp.float32
        ).astype(jnp.bfloat16)

    return lax.map(one_block, blocked).reshape(queries.shape)


def general_device(
    image,
    modulation,
    query_key_value_weight,
    pooled_down_factor,
    pooled_up_factor,
    request_adapter,
    adapter_slot_table,
    row_request,
    text_key_value,
    query_key_gain,
):
    seq_index = lax.axis_index("seq")
    all_requests = request_adapter.shape[0]
    local_pool_slice = pooled_down_factor.shape[0]
    pool_total = adapter_slot_table.shape[0]
    heads_local = query_key_value_weight.shape[1] // (3 * HEAD_SIZE)
    text_local = text_key_value.shape[1]
    modulated = layer_modulate(image, modulation)
    request_match = row_request[:, None] == jnp.arange(all_requests, dtype=jnp.int32)[None, :]
    chosen_ids = jnp.sum(jnp.where(request_match, request_adapter[None, :], 0), axis=1)
    slot_match = chosen_ids[:, None] == jnp.arange(pool_total, dtype=jnp.int32)[None, :]
    slots = jnp.sum(jnp.where(slot_match, adapter_slot_table[None, :], 0), axis=1)
    owned = slots // local_pool_slice == seq_index
    local_match = (slots % local_pool_slice)[:, None] == jnp.arange(
        local_pool_slice, dtype=jnp.int32
    )[None, :]
    slot_picker = (owned[:, None] & local_match).astype(jnp.bfloat16)
    up_terms = jnp.einsum(
        "eq,qfx->efx", slot_picker, pooled_up_factor, preferred_element_type=jnp.float32
    ).astype(jnp.bfloat16)
    down_terms = jnp.einsum(
        "mv,vna->mna", slot_picker, pooled_down_factor, preferred_element_type=jnp.float32
    ).astype(jnp.bfloat16)
    down_fetched, up_fetched = (
        lax.psum(down_terms, "seq").astype(jnp.float32),
        lax.psum(up_terms, "seq").astype(jnp.float32),
    )
    down_fetched = down_fetched.astype(jnp.bfloat16)
    up_fetched = up_fetched.astype(jnp.bfloat16)
    block_rows = lax.all_gather(modulated, "adapt", axis=0, tiled=True)
    shrunk = jnp.einsum(
        "rtd,rdk->rtk", block_rows, down_fetched, preferred_element_type=jnp.float32
    ).astype(jnp.bfloat16)
    frozen = jnp.einsum(
        "rtd,dc->rtc", block_rows, query_key_value_weight, preferred_element_type=jnp.float32
    )
    qkv = frozen + jnp.einsum(
        "rtk,rkc->rtc", shrunk, up_fetched, preferred_element_type=jnp.float32
    )
    token_local = qkv.shape[1]
    qkv = qkv.reshape(all_requests, token_local, heads_local, 3, HEAD_SIZE)
    queries = rms_scale(qkv[:, :, :, 0], query_key_gain[0]).astype(jnp.bfloat16)
    image_keys = rms_scale(qkv[:, :, :, 1], query_key_gain[1]).astype(jnp.bfloat16)
    image_values = qkv[:, :, :, 2].astype(jnp.bfloat16)
    image_pairs = jnp.transpose(jnp.stack([image_keys, image_values], axis=3), (0, 2, 1, 3, 4))
    text_pairs = jnp.transpose(
        text_key_value.reshape(all_requests, text_local, 2, heads_local, HEAD_SIZE), (0, 3, 1, 2, 4)
    )
    joined = jnp.concatenate([image_pairs, text_pairs], axis=2)
    joined = joined.reshape(all_requests * heads_local, token_local + text_local, 2, HEAD_SIZE)
    queries = jnp.transpose(queries, (0, 2, 1, 3)).reshape(
        all_requests * heads_local, token_local, HEAD_SIZE
    )
    query_items, joined_items = (
        lax.all_to_all(queries, "seq", split_axis=0, concat_axis=1, tiled=True),
        lax.all_to_all(joined, "seq", split_axis=0, concat_axis=1, tiled=True),
    )
    attended = lax.map(attend_item, (query_items, joined_items))
    returned = lax.all_to_all(attended, "seq", split_axis=1, concat_axis=0, tiled=True)
    returned = returned.reshape(all_requests, heads_local, token_local, HEAD_SIZE)
    return jnp.transpose(returned, (0, 2, 1, 3)).reshape(
        all_requests, token_local, heads_local * HEAD_SIZE
    )


BF16 = jnp.bfloat16
ROUNDS = 8
EARLY = 6
FIRST = 2
LAG = 4
F32 = jnp.float32
ANY = pl.BlockSpec(memory_space=pl.ANY)
WHOLE = pl.BlockSpec(memory_space=pltpu.VMEM)


def flipped(index, k):
    low = 1 - 2 * lax.rem(index, 2) if k % 2 else 0
    high = 2 - 4 * (index // 2) if k // 2 else 0
    return index + low + high


def block_kernel(
    image, modulation, weight, down, up, gain, text,
    out, tok,
    weight_held, mod, rows_held, q_held, k_held, v_held, txt,
    up_near, down_near, up_sent, down_sent, up_far, down_far, down_all, down_whole,
    image_sem, weight_sem, load_sem,
    tok_send, tok_recv, side_send, side_recv, across_send, across_recv, last_send, last_recv,
    near_send, near_recv, far_send, far_recv, spread_send, spread_recv,
    text_send, text_recv, out_send, out_recv,
):
    s = lax.axis_index("seq")
    a = lax.axis_index("adapt")
    x = a // 2
    c = lax.rem(a, 2)
    me = s * 4 + a
    sibling = {"seq": s, "adapt": 2 * x + 1 - c}
    partner = {"seq": s, "adapt": 2 * (1 - x) + c}
    request_row = (x, 1 - x)
    piece_rows = tok.shape[4]
    width = tok.shape[5]
    chunk_rows = 16 * piece_rows
    head_columns = q_held.shape[5]
    heads = head_columns // HEAD_SIZE
    token_local = 2 * ROUNDS * piece_rows
    half_rows = ROUNDS * piece_rows
    text_rows = 4 * txt.shape[2]

    def remote(source, target, send, recv, device):
        return pltpu.make_async_remote_copy(
            src_ref=source, dst_ref=target, send_sem=send, recv_sem=recv,
            device_id=device, device_id_type=pl.DeviceIdType.MESH,
        )

    weight_copy = pltpu.make_async_copy(weight, weight_held, weight_sem)

    def image_copy(n):
        return pltpu.make_async_copy(image.at[:, :, n], mod.at[:, :, n], image_sem.at[n])

    for n in range(ROUNDS):
        image_copy(n).start()
    weight_copy.start()

    barrier = pltpu.get_barrier_semaphore()
    for k in range(1, 16):
        other = lax.rem(me + k, 16)
        pl.semaphore_signal(
            barrier, inc=1, device_id={"seq": other // 4, "adapt": lax.rem(other, 4)},
            device_id_type=pl.DeviceIdType.MESH,
        )
    pl.semaphore_wait(barrier, 15)

    def near_copies():
        to = {"seq": flipped(s, 1), "adapt": a}
        copies = []
        for n, k in enumerate((1, 3)):
            place = flipped(s, k)
            copies.append(remote(up.at[:, place], up_near.at[n], near_send.at[n], near_recv.at[n], to))
            copies.append(
                remote(down.at[:, place], down_near.at[n], near_send.at[2 + n], near_recv.at[2 + n], to)
            )
        return copies

    def far_copies():
        to = {"seq": flipped(s, 2), "adapt": a}
        return [
            remote(up_sent, up_far, far_send.at[0], far_recv.at[0], to),
            remote(down_sent, down_far, far_send.at[1], far_recv.at[1], to),
        ]

    def spread_copy(k):
        return remote(
            down_all.at[a], down_all.at[a], spread_send.at[k], spread_recv.at[k],
            {"seq": s, "adapt": flipped(a, k)},
        )

    def spread_in(k):
        other = flipped(a, k)
        return remote(
            down_all.at[other], down_all.at[other], spread_send.at[k], spread_recv.at[k], sibling
        )

    def handed(n, j, h):
        place = 2 * c + j
        mine = jnp.logical_and(place == s, c == h)
        recv = tok_recv.at[n, s]
        source, target = mod.at[j, h, n], tok.at[0, s, h, n]
        away = remote(
            source, target, tok_send.at[n, 2 * j + h], recv, {"seq": place, "adapt": 2 * x + h}
        )
        return mine, away, pltpu.make_async_copy(source, target, recv)

    def start_round(n):
        for j in range(2):
            for h in range(2):
                mine, away, here = handed(n, j, h)

                @pl.when(mine)
                def _():
                    here.start()

                @pl.when(jnp.logical_not(mine))
                def _():
                    away.start()

    def end_round(n):
        for j in range(2):
            for h in range(2):
                mine, away, _ = handed(n, j, h)

                @pl.when(jnp.logical_not(mine))
                def _():
                    away.wait_send()

    def modulate_round(n):
        image_copy(n).wait()
        step_rows = 16
        parts = piece_rows // step_rows

        def one(b, carry):
            j = b // (2 * parts)
            h = lax.rem(b // parts, 2)
            rows = pl.ds(pl.multiple_of(lax.rem(b, parts) * step_rows, step_rows), step_rows)
            widened = mod[j, h, n, rows, :].astype(F32)
            centre = widened - jnp.mean(widened, axis=-1, keepdims=True)
            variance = jnp.mean(centre * centre, axis=-1, keepdims=True)
            normed = centre * lax.rsqrt(variance + 1e-06)
            shift = modulation[j, 0:1, :]
            scale = modulation[j, 1:2, :]
            mod[j, h, n, rows, :] = ((1.0 + scale) * normed + shift).astype(BF16)
            return carry

        lax.fori_loop(0, 4 * parts, one, 0)

    def piece(i, n, k, core):
        return tok.at[i, flipped(s, k), core, n]

    def first(n, k):
        here = piece(0, n, k, c)
        return remote(here, here, tok_send.at[n, 0], tok_recv.at[n, flipped(s, k)], sibling)

    def side(n, k):
        here = piece(0, n, k, c)
        return remote(here, here, side_send.at[n, k], side_recv.at[n, k], sibling)

    def side_in(n, k):
        there = piece(0, n, k, 1 - c)
        return remote(there, there, side_send.at[n, k], side_recv.at[n, k], sibling)

    def across(n, k):
        return remote(
            piece(0, n, k, c), piece(1, n, k, c), across_send.at[n, k], across_recv.at[n, k], partner
        )

    def last(n, k):
        here = piece(1, n, k, c)
        return remote(here, here, last_send.at[n, k], last_recv.at[n, k], sibling)

    def last_in(n, k):
        there = piece(1, n, k, 1 - c)
        return remote(there, there, last_send.at[n, k], last_recv.at[n, k], sibling)

    def text_copy(i, k):
        place = flipped(s, k)
        row = request_row[i]
        return remote(
            text.at[row, place], txt.at[i, s], text_send.at[i, k], text_recv.at[i, k],
            {"seq": place, "adapt": a},
        )

    def text_in(i, k):
        place = flipped(s, k)
        return remote(
            txt.at[i, place], txt.at[i, place], text_send.at[i, k], text_recv.at[i, k], sibling
        )

    def own_text(i):
        return pltpu.make_async_copy(text.at[request_row[i], s], txt.at[i, s], text_recv.at[i, 0])

    for i in range(2):
        own_text(i).start()

    def opening(n, carry):
        modulate_round(n)

        @pl.when(n < EARLY)
        def _():
            start_round(n)

        @pl.when(n == FIRST - 1)
        def _():
            for copy in near_copies():
                copy.start()

        return carry

    lax.fori_loop(0, ROUNDS, opening, 0)

    for copy in near_copies():
        copy.wait_recv()
    away = flipped(s, 2)
    up_sent[...] = up[:, away] + up_near[1]
    down_sent[...] = down[:, away] + down_near[1]
    for copy in far_copies():
        copy.start()
    up_near[0] = up[:, s] + up_near[0]
    down_near[0] = down[:, s] + down_near[0]

    def start_rest(n, carry):
        start_round(n)
        return carry

    lax.fori_loop(EARLY, ROUNDS, start_rest, 0)
    for i in range(2):
        for k in (2, 3, 1):
            text_copy(i, k).start()

    def pass_on(n):
        for k in range(4):
            first(n, k).wait_recv()
            across(n, k).start()
            side(n, k).start()

    def load(i, n):
        return pltpu.make_async_copy(
            tok.at[i, :, :, pl.ds(2 * n, 2)], rows_held.at[i], load_sem.at[i]
        )

    def project(i, n):
        rows = rows_held[i].reshape(chunk_rows, width)
        row = request_row[i]
        shrunk = lax.dot_general(
            rows, down_whole[row], (((1,), (1,)), ((), ())), preferred_element_type=F32
        ).astype(BF16)
        wide = 6 * HEAD_SIZE
        for part in range(weight_held.shape[1] // wide):
            columns = slice(part * wide, (part + 1) * wide)
            qkv = jnp.dot(rows, weight_held[:, columns], preferred_element_type=F32)
            qkv = qkv + jnp.dot(shrunk, up_far[row, :, columns], preferred_element_type=F32)
            for h in range(2):
                head = slice((2 * part + h) * HEAD_SIZE, (2 * part + h + 1) * HEAD_SIZE)
                q, k, v = (
                    qkv[:, (3 * h + m) * HEAD_SIZE : (3 * h + m + 1) * HEAD_SIZE] for m in range(3)
                )
                shape = (4, 2, 2, piece_rows, HEAD_SIZE)
                pair = pl.ds(2 * n, 2)
                q_held[i, :, :, pair, :, head] = rms_scale(q, gain[0:1, :]).astype(BF16).reshape(shape)
                k_held[i, :, :, pair, :, head] = rms_scale(k, gain[1:2, :]).astype(BF16).reshape(shape)
                v_held[i, :, :, pair, :, head] = v.astype(BF16).reshape(shape)

    def hand_over(n):
        for k in range(4):
            across(n, k).wait_recv()
            last(n, k).start()

    def lead(n, carry):
        pass_on(n)

        @pl.when(n > 1)
        def _():
            hand_over(n - 2)

        return carry

    lax.fori_loop(0, LAG, lead, 0)
    for copy in far_copies():
        copy.wait_recv()
    up_far[...] = up_near[0] + up_far[...]
    down_all[a] = down_near[0] + down_far[...]
    for k in range(1, 4):
        spread_copy(k).start()
    weight_copy.wait()

    def stage(n, carry):
        @pl.when(n < ROUNDS)
        def _():
            pass_on(n)

        @pl.when(n == LAG)
        def _():
            for k in range(1, 4):
                spread_in(k).wait_recv()
            share = down_all.shape[3]
            for k in range(4):
                down_whole[:, :, k * share : (k + 1) * share] = down_all[k]

        hand_over(n - 2)

        @pl.when(n == ROUNDS)
        def _():
            hand_over(ROUNDS - 1)

        @pl.when(n < ROUNDS)
        def _():
            for m in range(2):
                for k in range(4):
                    side_in(2 * (n - LAG) + m, k).wait_recv()
            load(0, n - LAG).start()

        @pl.when(n > LAG)
        def _():
            for m in range(2):
                for k in range(4):
                    last_in(2 * (n - LAG - 1) + m, k).wait_recv()
            load(1, n - LAG - 1).start()

        @pl.when(n < ROUNDS)
        def _():
            load(0, n - LAG).wait()
            project(0, n - LAG)

        @pl.when(n > LAG)
        def _():
            load(1, n - LAG - 1).wait()
            project(1, n - LAG - 1)

        return carry

    lax.fori_loop(LAG, ROUNDS + 1, stage, 0)

    factor = math.log2(math.e) / math.sqrt(HEAD_SIZE)

    def target(step):
        return jnp.where(
            step == 3, s,
            jnp.where(step == 2, flipped(s, 1), jnp.where(step == 1, flipped(s, 3), flipped(s, 2))),
        )

    def out_copy(i, part, slot, row_from, place):
        row = 4 * jnp.where(i == 0, x, 1 - x) + row_from
        return remote(
            q_held.at[i, place, part], out.at[row, part], out_send.at[slot], out_recv.at[slot],
            {"seq": place, "adapt": a},
        )

    def own_out(i, part, slot):
        row = 4 * jnp.where(i == 0, x, 1 - x) + s
        return pltpu.make_async_copy(q_held.at[i, s, part], out.at[row, part], out_recv.at[slot])

    def placed(slot):
        far = slot < 8
        i = jnp.where(far, slot // 4, lax.rem(slot // 2, 2))
        step = jnp.where(far, lax.rem(slot // 2, 2), slot // 4)
        return i, step, lax.rem(slot, 2), target(step)

    def attend_step(slot, carry):
        i, step, part, place = placed(slot)

        for r in range(2):
            @pl.when(slot == 4 * r)
            def _():
                own_text(r).wait()
                for k in range(1, 4):
                    text_in(r, k).wait_recv()

        def scores(h):
            head = slice(h * HEAD_SIZE, (h + 1) * HEAD_SIZE)
            query = q_held[i, place, part, :, :, head].reshape(half_rows, HEAD_SIZE)
            image_keys = k_held[i, :, :, :, :, head].reshape(4 * token_local, HEAD_SIZE)
            text_keys = txt[i, :, :, head].reshape(text_rows, HEAD_SIZE)
            return tuple(
                lax.dot_general(
                    query, key_rows, (((1,), (1,)), ((), ())), preferred_element_type=F32
                )
                for key_rows in (image_keys, text_keys)
            )

        ready = scores(0)
        for h in range(heads):
            one, two = ready
            if h + 1 < heads:
                ready = scores(h + 1)
            head = slice(h * HEAD_SIZE, (h + 1) * HEAD_SIZE)
            value_head = slice(head_columns + h * HEAD_SIZE, head_columns + (h + 1) * HEAD_SIZE)
            highest = jnp.maximum(
                jnp.max(one, axis=-1, keepdims=True), jnp.max(two, axis=-1, keepdims=True)
            )
            one = jnp.exp2((one - highest) * factor)
            two = jnp.exp2((two - highest) * factor)
            share = 1.0 / (jnp.sum(one, axis=-1, keepdims=True) + jnp.sum(two, axis=-1, keepdims=True))
            image_values = v_held[i, :, :, :, :, head].reshape(4 * token_local, HEAD_SIZE)
            text_values = txt[i, :, :, value_head].reshape(text_rows, HEAD_SIZE)
            total = jnp.dot((one * share).astype(BF16), image_values, preferred_element_type=F32)
            total = total + jnp.dot(
                (two * share).astype(BF16), text_values, preferred_element_type=F32
            )
            q_held[i, place, part, :, :, head] = total.astype(BF16).reshape(
                ROUNDS, piece_rows, HEAD_SIZE
            )

        @pl.when(step == 3)
        def _():
            own_out(i, part, slot).start()

        @pl.when(step < 3)
        def _():
            out_copy(i, part, slot, s, place).start()

        return carry

    lax.fori_loop(0, 16, attend_step, 0)

    def finish_round(n, carry):
        end_round(n)
        for k in range(4):
            side(n, k).wait_send()
            across(n, k).wait_send()
            last(n, k).wait_send()
        return carry

    lax.fori_loop(0, ROUNDS, finish_round, 0)
    for copy in near_copies() + far_copies():
        copy.wait_send()
    for k in range(1, 4):
        spread_copy(k).wait_send()
        for i in range(2):
            text_copy(i, k).wait_send()

    def finish_out(slot, carry):
        i, step, part, place = placed(slot)

        @pl.when(step == 3)
        def _():
            own_out(i, part, slot).wait()

        @pl.when(step < 3)
        def _():
            out_copy(i, part, slot, place, place).wait()

        return carry

    lax.fori_loop(0, 16, finish_out, 0)


def on_device(
    image,
    modulation,
    query_key_value_weight,
    pooled_down_factor,
    pooled_up_factor,
    request_adapter,
    adapter_slot_table,
    row_request,
    text_key_value,
    query_key_gain,
):
    seq_index = lax.axis_index("seq")
    all_requests = request_adapter.shape[0]
    pool_local, width, rank = pooled_down_factor.shape
    pool_total = adapter_slot_table.shape[0]
    columns = query_key_value_weight.shape[1]
    head_columns = columns // 3
    text_local = text_key_value.shape[1]
    token_local = image.shape[1]
    request_match = row_request[:, None] == jnp.arange(all_requests, dtype=jnp.int32)[None, :]
    chosen_ids = jnp.sum(jnp.where(request_match, request_adapter[None, :], 0), axis=1)
    slot_match = chosen_ids[:, None] == jnp.arange(pool_total, dtype=jnp.int32)[None, :]
    slots = jnp.sum(jnp.where(slot_match, adapter_slot_table[None, :], 0), axis=1)
    owned = slots // pool_local == seq_index
    local_match = (slots % pool_local)[:, None] == jnp.arange(pool_local, dtype=jnp.int32)[None, :]
    slot_picker = (owned[:, None] & local_match).astype(BF16)
    share = width // 4
    down_part = lax.dynamic_slice_in_dim(
        pooled_down_factor, lax.axis_index("adapt") * share, share, axis=1
    )
    down_terms = jnp.einsum(
        "mv,vna->man", slot_picker, down_part, preferred_element_type=F32
    ).astype(BF16)
    up_terms = jnp.einsum(
        "eq,qfx->efx", slot_picker, pooled_up_factor, preferred_element_type=F32
    ).astype(BF16)

    piece_rows = token_local // (2 * ROUNDS)
    held = pltpu.VMEM((2, 4, 2, ROUNDS, piece_rows, head_columns), BF16)

    def dma(*shape):
        return pltpu.SemaphoreType.DMA(shape)

    out, _ = pl.pallas_call(
        block_kernel,
        out_shape=(
            jax.ShapeDtypeStruct((all_requests, 2, ROUNDS, piece_rows, head_columns), BF16),
            jax.ShapeDtypeStruct((2, 4, 2, ROUNDS, piece_rows, width), BF16),
        ),
        in_specs=[ANY, WHOLE, ANY, WHOLE, WHOLE, WHOLE, ANY],
        out_specs=(ANY, ANY),
        scratch_shapes=[
            pltpu.VMEM((width, columns), BF16),
            pltpu.VMEM((2, 2, ROUNDS, piece_rows, width), BF16),
            pltpu.VMEM((2, 4, 2, 2, piece_rows, width), BF16),
            held, held, held,
            pltpu.VMEM((2, 4, text_local, 2 * head_columns), BF16),
            pltpu.VMEM((2, 2, rank, columns), BF16),
            pltpu.VMEM((2, 2, rank, share), BF16),
            pltpu.VMEM((2, rank, columns), BF16),
            pltpu.VMEM((2, rank, share), BF16),
            pltpu.VMEM((2, rank, columns), BF16),
            pltpu.VMEM((2, rank, share), BF16),
            pltpu.VMEM((4, 2, rank, share), BF16),
            pltpu.VMEM((2, rank, width), BF16),
            dma(ROUNDS), dma(), dma(2),
        ]
        + [dma(ROUNDS, 4)] * 8
        + [dma(4)] * 2 + [dma(2)] * 2 + [dma(4)] * 2
        + [dma(2, 4)] * 2 + [dma(16)] * 2,
        compiler_params=pltpu.CompilerParams(
            collective_id=0, has_side_effects=True, vmem_limit_bytes=58 * 2**20
        ),
        name="block",
    )(
        image.reshape(2, 2, ROUNDS, piece_rows, width),
        modulation,
        query_key_value_weight,
        down_terms.reshape(2, 4, rank, share),
        up_terms.reshape(2, 4, rank, columns),
        query_key_gain,
        text_key_value.reshape(2, 4, text_local, 2 * head_columns),
    )
    return out.reshape(all_requests, token_local, head_columns)


def solution(mesh):
    in_specs = (
        P(("groups", "adapt"), "seq", None),
        P(("groups", "adapt"), None, None),
        P(None, "adapt"),
        P("seq", None, None),
        P("seq", None, "adapt"),
        P("groups"),
        P(),
        P("groups"),
        P("groups", "seq", None, "adapt"),
        P(),
    )
    out_specs = P("groups", "seq", "adapt")
    def chosen(*operands):
        image, request_adapter = operands[0], operands[5]
        fits = (
            mesh.shape["seq"] == 4
            and mesh.shape["adapt"] == 4
            and request_adapter.shape[0] == 8
            and image.shape[0] == 2
            and operands[2].shape[1] % (6 * HEAD_SIZE) == 0
            and image.shape[1] % 256 == 0
            and image.shape[2] % 512 == 0
        )
        return (on_device if fits else general_device)(*operands)

    return jax.shard_map(
        chosen, mesh=mesh, in_specs=in_specs, out_specs=out_specs, check_vma=False
    )
```

```python
import functools
import math

import jax
import jax.numpy as jnp
from jax import lax
from jax.experimental import pallas as pl
from jax.experimental.pallas import tpu as pltpu
from jax.sharding import PartitionSpec as P

HEAD_SIZE = 128


def layer_modulate(image, modulation):
    widened = image.astype(jnp.float32)
    centre = widened - jnp.mean(widened, axis=-1, keepdims=True)
    variance = jnp.mean(centre * centre, axis=-1, keepdims=True)
    normed = centre * lax.rsqrt(variance + 1e-06)
    return ((1.0 + modulation[:, 1, None, :]) * normed + modulation[:, 0, None, :]).astype(
        jnp.bfloat16
    )


def rms_scale(values, gain):
    return values * lax.rsqrt(jnp.mean(values * values, axis=-1, keepdims=True) + 1e-06) * gain


def attend_item(operands):
    queries, joined = operands
    key_rows = joined[:, 0]
    value_rows = joined[:, 1]
    query_count = queries.shape[0]
    block = math.gcd(query_count, 512)
    inverse = 1.0 / math.sqrt(queries.shape[-1])
    blocked = queries.reshape(query_count // block, block, queries.shape[-1])

    def one_block(block_rows):
        scores = (
            lax.dot_general(
                block_rows, key_rows, (((1,), (1,)), ((), ())), preferred_element_type=jnp.float32
            )
            * inverse
        )
        highest = jnp.max(scores, axis=-1, keepdims=True)
        weights = jnp.exp(scores - highest)
        weights = weights / jnp.sum(weights, axis=-1, keepdims=True)
        return jnp.dot(
            weights.astype(jnp.bfloat16), value_rows, preferred_element_type=jnp.float32
        ).astype(jnp.bfloat16)

    return lax.map(one_block, blocked).reshape(queries.shape)


def general_device(
    image,
    modulation,
    query_key_value_weight,
    pooled_down_factor,
    pooled_up_factor,
    request_adapter,
    adapter_slot_table,
    row_request,
    text_key_value,
    query_key_gain,
):
    seq_index = lax.axis_index("seq")
    all_requests = request_adapter.shape[0]
    local_pool_slice = pooled_down_factor.shape[0]
    pool_total = adapter_slot_table.shape[0]
    heads_local = query_key_value_weight.shape[1] // (3 * HEAD_SIZE)
    text_local = text_key_value.shape[1]
    modulated = layer_modulate(image, modulation)
    request_match = row_request[:, None] == jnp.arange(all_requests, dtype=jnp.int32)[None, :]
    chosen_ids = jnp.sum(jnp.where(request_match, request_adapter[None, :], 0), axis=1)
    slot_match = chosen_ids[:, None] == jnp.arange(pool_total, dtype=jnp.int32)[None, :]
    slots = jnp.sum(jnp.where(slot_match, adapter_slot_table[None, :], 0), axis=1)
    owned = slots // local_pool_slice == seq_index
    local_match = (slots % local_pool_slice)[:, None] == jnp.arange(
        local_pool_slice, dtype=jnp.int32
    )[None, :]
    slot_picker = (owned[:, None] & local_match).astype(jnp.bfloat16)
    up_terms = jnp.einsum(
        "eq,qfx->efx", slot_picker, pooled_up_factor, preferred_element_type=jnp.float32
    ).astype(jnp.bfloat16)
    down_terms = jnp.einsum(
        "mv,vna->mna", slot_picker, pooled_down_factor, preferred_element_type=jnp.float32
    ).astype(jnp.bfloat16)
    down_fetched, up_fetched = (
        lax.psum(down_terms, "seq").astype(jnp.float32),
        lax.psum(up_terms, "seq").astype(jnp.float32),
    )
    down_fetched = down_fetched.astype(jnp.bfloat16)
    up_fetched = up_fetched.astype(jnp.bfloat16)
    block_rows = lax.all_gather(modulated, "adapt", axis=0, tiled=True)
    shrunk = jnp.einsum(
        "rtd,rdk->rtk", block_rows, down_fetched, preferred_element_type=jnp.float32
    ).astype(jnp.bfloat16)
    frozen = jnp.einsum(
        "rtd,dc->rtc", block_rows, query_key_value_weight, preferred_element_type=jnp.float32
    )
    qkv = frozen + jnp.einsum(
        "rtk,rkc->rtc", shrunk, up_fetched, preferred_element_type=jnp.float32
    )
    token_local = qkv.shape[1]
    qkv = qkv.reshape(all_requests, token_local, heads_local, 3, HEAD_SIZE)
    queries = rms_scale(qkv[:, :, :, 0], query_key_gain[0]).astype(jnp.bfloat16)
    image_keys = rms_scale(qkv[:, :, :, 1], query_key_gain[1]).astype(jnp.bfloat16)
    image_values = qkv[:, :, :, 2].astype(jnp.bfloat16)
    image_pairs = jnp.transpose(jnp.stack([image_keys, image_values], axis=3), (0, 2, 1, 3, 4))
    text_pairs = jnp.transpose(
        text_key_value.reshape(all_requests, text_local, 2, heads_local, HEAD_SIZE), (0, 3, 1, 2, 4)
    )
    joined = jnp.concatenate([image_pairs, text_pairs], axis=2)
    joined = joined.reshape(all_requests * heads_local, token_local + text_local, 2, HEAD_SIZE)
    queries = jnp.transpose(queries, (0, 2, 1, 3)).reshape(
        all_requests * heads_local, token_local, HEAD_SIZE
    )
    query_items, joined_items = (
        lax.all_to_all(queries, "seq", split_axis=0, concat_axis=1, tiled=True),
        lax.all_to_all(joined, "seq", split_axis=0, concat_axis=1, tiled=True),
    )
    attended = lax.map(attend_item, (query_items, joined_items))
    returned = lax.all_to_all(attended, "seq", split_axis=1, concat_axis=0, tiled=True)
    returned = returned.reshape(all_requests, heads_local, token_local, HEAD_SIZE)
    return jnp.transpose(returned, (0, 2, 1, 3)).reshape(
        all_requests, token_local, heads_local * HEAD_SIZE
    )


BF16 = jnp.bfloat16
ROUNDS = 8
EARLY = 4
FIRST = 1
LAG = 4
F32 = jnp.float32
ANY = pl.BlockSpec(memory_space=pl.ANY)
WHOLE = pl.BlockSpec(memory_space=pltpu.VMEM)
SCALARS = pl.BlockSpec(memory_space=pltpu.SMEM)


def flipped(index, k):
    low = 1 - 2 * lax.rem(index, 2) if k % 2 else 0
    high = 2 - 4 * (index // 2) if k // 2 else 0
    return index + low + high


def block_kernel(
    image, modulation, weight, down_pool, up_pool, gain, text, adapter_of, slot_of, request_of,
    out, tok,
    weight_held, mod, rows_held, q_held, k_held, v_held, txt,
    up, down, up_out, down_out, up_near, down_near, up_sent, down_sent, up_far, down_far, down_all, down_whole,
    image_sem, weight_sem, load_sem, pool_sem,
    tok_send, tok_recv, side_send, side_recv, across_send, across_recv, last_send, last_recv,
    near_send, near_recv, far_send, far_recv, spread_send, spread_recv,
    text_send, text_recv, out_send, out_recv,
):
    s = lax.axis_index("seq")
    a = lax.axis_index("adapt")
    x = a // 2
    c = lax.rem(a, 2)
    me = s * 4 + a
    sibling = {"seq": s, "adapt": 2 * x + 1 - c}
    partner = {"seq": s, "adapt": 2 * (1 - x) + c}
    request_row = (x, 1 - x)
    piece_rows = tok.shape[4]
    width = tok.shape[5]
    chunk_rows = 16 * piece_rows
    head_columns = q_held.shape[5]
    heads = head_columns // HEAD_SIZE
    token_local = 2 * ROUNDS * piece_rows
    half_rows = ROUNDS * piece_rows
    text_rows = 4 * txt.shape[2]

    def remote(source, target, send, recv, device):
        return pltpu.make_async_remote_copy(
            src_ref=source, dst_ref=target, send_sem=send, recv_sem=recv,
            device_id=device, device_id_type=pl.DeviceIdType.MESH,
        )

    weight_copy = pltpu.make_async_copy(weight, weight_held, weight_sem)

    def image_copy(n):
        return pltpu.make_async_copy(image.at[:, :, n], mod.at[:, :, n], image_sem.at[n])

    for n in range(ROUNDS):
        image_copy(n).start()
    share = down_all.shape[3]
    quarter = pl.ds(pl.multiple_of(a * share, HEAD_SIZE), share)
    pool_copies = (
        pltpu.make_async_copy(down_pool.at[:, :, quarter], down, pool_sem.at[0]),
        pltpu.make_async_copy(up_pool, up, pool_sem.at[1]),
    )
    for copy in pool_copies:
        copy.start()
    weight_copy.start()

    barrier = pltpu.get_barrier_semaphore()
    for k in range(1, 16):
        other = lax.rem(me + k, 16)
        pl.semaphore_signal(
            barrier, inc=1, device_id={"seq": other // 4, "adapt": lax.rem(other, 4)},
            device_id_type=pl.DeviceIdType.MESH,
        )
    pl.semaphore_wait(barrier, 15)

    pool_local = up.shape[0]

    def picked(pool, place):
        terms = []
        for r in range(2):
            slot = slot_of[adapter_of[request_of[4 * r + place]]]
            mine = jnp.where(slot // pool_local == s, 1.0, 0.0)
            terms.append((pool[lax.rem(slot, pool_local)].astype(F32) * mine).astype(BF16))
        return terms

    def near_copies():
        to = {"seq": flipped(s, 1), "adapt": a}
        copies = []
        for n in range(2):
            copies.append(remote(up_out.at[n], up_near.at[n], near_send.at[n], near_recv.at[n], to))
            copies.append(
                remote(down_out.at[n], down_near.at[n], near_send.at[2 + n], near_recv.at[2 + n], to)
            )
        return copies

    def far_copies():
        to = {"seq": flipped(s, 2), "adapt": a}
        return [
            remote(up_sent, up_far, far_send.at[0], far_recv.at[0], to),
            remote(down_sent, down_far, far_send.at[1], far_recv.at[1], to),
        ]

    def spread_copy(k):
        return remote(
            down_all.at[a], down_all.at[a], spread_send.at[k], spread_recv.at[k],
            {"seq": s, "adapt": flipped(a, k)},
        )

    def spread_in(k):
        other = flipped(a, k)
        return remote(
            down_all.at[other], down_all.at[other], spread_send.at[k], spread_recv.at[k], sibling
        )

    def handed(n, j, h):
        place = 2 * c + j
        mine = jnp.logical_and(place == s, c == h)
        recv = tok_recv.at[n, s]
        source, target = mod.at[j, h, n], tok.at[0, s, h, n]
        away = remote(
            source, target, tok_send.at[n, 2 * j + h], recv, {"seq": place, "adapt": 2 * x + h}
        )
        return mine, away, pltpu.make_async_copy(source, target, recv)

    def start_round(n):
        for j in range(2):
            for h in range(2):
                mine, away, here = handed(n, j, h)

                @pl.when(mine)
                def _():
                    here.start()

                @pl.when(jnp.logical_not(mine))
                def _():
                    away.start()

    def end_round(n):
        for j in range(2):
            for h in range(2):
                mine, away, _ = handed(n, j, h)

                @pl.when(jnp.logical_not(mine))
                def _():
                    away.wait_send()

    def modulate_round(n):
        image_copy(n).wait()
        step_rows = 16
        parts = piece_rows // step_rows

        def one(b, carry):
            j = b // (2 * parts)
            h = lax.rem(b // parts, 2)
            rows = pl.ds(pl.multiple_of(lax.rem(b, parts) * step_rows, step_rows), step_rows)
            widened = mod[j, h, n, rows, :].astype(F32)
            centre = widened - jnp.mean(widened, axis=-1, keepdims=True)
            variance = jnp.mean(centre * centre, axis=-1, keepdims=True)
            normed = centre * lax.rsqrt(variance + 1e-06)
            shift = modulation[j, 0:1, :]
            scale = modulation[j, 1:2, :]
            mod[j, h, n, rows, :] = ((1.0 + scale) * normed + shift).astype(BF16)
            return carry

        lax.fori_loop(0, 4 * parts, one, 0)

    def piece(i, n, k, core):
        return tok.at[i, flipped(s, k), core, n]

    def first(n, k):
        here = piece(0, n, k, c)
        return remote(here, here, tok_send.at[n, 0], tok_recv.at[n, flipped(s, k)], sibling)

    def side(n, k):
        here = piece(0, n, k, c)
        return remote(here, here, side_send.at[n, k], side_recv.at[n, k], sibling)

    def side_in(n, k):
        there = piece(0, n, k, 1 - c)
        return remote(there, there, side_send.at[n, k], side_recv.at[n, k], sibling)

    def across(n, k):
        return remote(
            piece(0, n, k, c), piece(1, n, k, c), across_send.at[n, k], across_recv.at[n, k], partner
        )

    def last(n, k):
        here = piece(1, n, k, c)
        return remote(here, here, last_send.at[n, k], last_recv.at[n, k], sibling)

    def last_in(n, k):
        there = piece(1, n, k, 1 - c)
        return remote(there, there, last_send.at[n, k], last_recv.at[n, k], sibling)

    def text_copy(i, k):
        place = flipped(s, k)
        row = request_row[i]
        return remote(
            text.at[row, place], txt.at[i, s], text_send.at[i, k], text_recv.at[i, k],
            {"seq": place, "adapt": a},
        )

    def text_in(i, k):
        place = flipped(s, k)
        return remote(
            txt.at[i, place], txt.at[i, place], text_send.at[i, k], text_recv.at[i, k], sibling
        )

    def own_text(i):
        return pltpu.make_async_copy(text.at[request_row[i], s], txt.at[i, s], text_recv.at[i, 0])

    for i in range(2):
        own_text(i).start()

    def opening(n, carry):
        modulate_round(n)

        @pl.when(n < EARLY)
        def _():
            start_round(n)

        @pl.when(n == FIRST - 1)
        def _():
            for copy in pool_copies:
                copy.wait()
            for m, k in enumerate((1, 3)):
                place = flipped(s, k)
                for r, (one, two) in enumerate(zip(picked(up, place), picked(down, place))):
                    up_out[m, r] = one
                    down_out[m, r] = two
            for copy in near_copies():
                copy.start()

        return carry

    lax.fori_loop(0, ROUNDS, opening, 0)

    def pass_on(n, sources=(1, 2, 3)):
        for k in sources:
            first(n, k).wait_recv()
            across(n, k).start()
            side(n, k).start()

    def pass_own(n, carry):
        pass_on(n, (0,))
        return carry

    lax.fori_loop(0, EARLY, pass_own, 0)

    for copy in near_copies():
        copy.wait_recv()
    away = flipped(s, 2)
    for r, (one, two) in enumerate(zip(picked(up, away), picked(down, away))):
        up_sent[r] = one + up_near[1, r]
        down_sent[r] = two + down_near[1, r]
    for copy in far_copies():
        copy.start()
    for r, (one, two) in enumerate(zip(picked(up, s), picked(down, s))):
        up_near[0, r] = one + up_near[0, r]
        down_near[0, r] = two + down_near[0, r]

    def start_rest(n, carry):
        start_round(n)
        return carry

    lax.fori_loop(EARLY, ROUNDS, start_rest, 0)
    for i in range(2):
        for k in (2, 3, 1):
            text_copy(i, k).start()
    lax.fori_loop(EARLY, ROUNDS, pass_own, 0)

    def load(i, n):
        return pltpu.make_async_copy(
            tok.at[i, :, :, pl.ds(2 * n, 2)], rows_held.at[i], load_sem.at[i]
        )

    def project(i, n):
        rows = rows_held[i].reshape(chunk_rows, width)
        row = request_row[i]
        shrunk = lax.dot_general(
            rows, down_whole[row], (((1,), (1,)), ((), ())), preferred_element_type=F32
        ).astype(BF16)
        wide = 6 * HEAD_SIZE
        for part in range(weight_held.shape[1] // wide):
            columns = slice(part * wide, (part + 1) * wide)
            qkv = jnp.dot(rows, weight_held[:, columns], preferred_element_type=F32)
            qkv = qkv + jnp.dot(shrunk, up_far[row, :, columns], preferred_element_type=F32)
            for h in range(2):
                head = slice((2 * part + h) * HEAD_SIZE, (2 * part + h + 1) * HEAD_SIZE)
                q, k, v = (
                    qkv[:, (3 * h + m) * HEAD_SIZE : (3 * h + m + 1) * HEAD_SIZE] for m in range(3)
                )
                shape = (4, 2, 2, piece_rows, HEAD_SIZE)
                pair = pl.ds(2 * n, 2)
                q_held[i, :, :, pair, :, head] = rms_scale(q, gain[0:1, :]).astype(BF16).reshape(shape)
                k_held[i, :, :, pair, :, head] = rms_scale(k, gain[1:2, :]).astype(BF16).reshape(shape)
                v_held[i, :, :, pair, :, head] = v.astype(BF16).reshape(shape)

    def hand_over(n):
        for k in range(4):
            across(n, k).wait_recv()
            last(n, k).start()

    def lead(n, carry):
        pass_on(n)

        @pl.when(n > 1)
        def _():
            hand_over(n - 2)

        return carry

    lax.fori_loop(0, LAG, lead, 0)
    for copy in far_copies():
        copy.wait_recv()
    up_far[...] = up_near[0] + up_far[...]
    down_all[a] = down_near[0] + down_far[...]
    for k in range(1, 4):
        spread_copy(k).start()
    weight_copy.wait()

    def stage(n, carry):
        @pl.when(n < ROUNDS)
        def _():
            pass_on(n)

        @pl.when(n == LAG)
        def _():
            for k in range(1, 4):
                spread_in(k).wait_recv()
            for k in range(4):
                down_whole[:, :, k * share : (k + 1) * share] = down_all[k]

        hand_over(n - 2)

        @pl.when(n == ROUNDS)
        def _():
            hand_over(ROUNDS - 1)

        @pl.when(n < ROUNDS)
        def _():
            for m in range(2):
                for k in range(4):
                    side_in(2 * (n - LAG) + m, k).wait_recv()
            load(0, n - LAG).start()

        @pl.when(n > LAG)
        def _():
            for m in range(2):
                for k in range(4):
                    last_in(2 * (n - LAG - 1) + m, k).wait_recv()
            load(1, n - LAG - 1).start()

        @pl.when(n < ROUNDS)
        def _():
            load(0, n - LAG).wait()
            project(0, n - LAG)

        @pl.when(n > LAG)
        def _():
            load(1, n - LAG - 1).wait()
            project(1, n - LAG - 1)

        return carry

    lax.fori_loop(LAG, ROUNDS + 1, stage, 0)

    factor = math.log2(math.e) / math.sqrt(HEAD_SIZE)

    def target(step):
        return jnp.where(
            step == 3, s,
            jnp.where(step == 2, flipped(s, 1), jnp.where(step == 1, flipped(s, 3), flipped(s, 2))),
        )

    def out_copy(i, part, slot, row_from, place):
        row = 4 * jnp.where(i == 0, x, 1 - x) + row_from
        return remote(
            q_held.at[i, place, part], out.at[row, part], out_send.at[slot], out_recv.at[slot],
            {"seq": place, "adapt": a},
        )

    def own_out(i, part, slot):
        row = 4 * jnp.where(i == 0, x, 1 - x) + s
        return pltpu.make_async_copy(q_held.at[i, s, part], out.at[row, part], out_recv.at[slot])

    def placed(slot):
        far = slot < 8
        i = jnp.where(far, slot // 4, lax.rem(slot // 2, 2))
        step = jnp.where(far, lax.rem(slot // 2, 2), slot // 4)
        return i, step, lax.rem(slot, 2), target(step)

    def attend_step(slot, carry):
        i, step, part, place = placed(slot)

        for r in range(2):
            @pl.when(slot == 4 * r)
            def _():
                own_text(r).wait()
                for k in range(1, 4):
                    text_in(r, k).wait_recv()

        def scores(h):
            head = slice(h * HEAD_SIZE, (h + 1) * HEAD_SIZE)
            query = q_held[i, place, part, :, :, head].reshape(half_rows, HEAD_SIZE)
            image_keys = k_held[i, :, :, :, :, head].reshape(4 * token_local, HEAD_SIZE)
            text_keys = txt[i, :, :, head].reshape(text_rows, HEAD_SIZE)
            return tuple(
                lax.dot_general(
                    query, key_rows, (((1,), (1,)), ((), ())), preferred_element_type=F32
                )
                for key_rows in (image_keys, text_keys)
            )

        ready = scores(0)
        for h in range(heads):
            one, two = ready
            if h + 1 < heads:
                ready = scores(h + 1)
            head = slice(h * HEAD_SIZE, (h + 1) * HEAD_SIZE)
            value_head = slice(head_columns + h * HEAD_SIZE, head_columns + (h + 1) * HEAD_SIZE)
            highest = jnp.maximum(
                jnp.max(one, axis=-1, keepdims=True), jnp.max(two, axis=-1, keepdims=True)
            )
            one = jnp.exp2((one - highest) * factor)
            two = jnp.exp2((two - highest) * factor)
            share = 1.0 / (jnp.sum(one, axis=-1, keepdims=True) + jnp.sum(two, axis=-1, keepdims=True))
            image_values = v_held[i, :, :, :, :, head].reshape(4 * token_local, HEAD_SIZE)
            text_values = txt[i, :, :, value_head].reshape(text_rows, HEAD_SIZE)
            total = jnp.dot((one * share).astype(BF16), image_values, preferred_element_type=F32)
            total = total + jnp.dot(
                (two * share).astype(BF16), text_values, preferred_element_type=F32
            )
            q_held[i, place, part, :, :, head] = total.astype(BF16).reshape(
                ROUNDS, piece_rows, HEAD_SIZE
            )

        @pl.when(step == 3)
        def _():
            own_out(i, part, slot).start()

        @pl.when(step < 3)
        def _():
            out_copy(i, part, slot, s, place).start()

        return carry

    lax.fori_loop(0, 16, attend_step, 0)

    def finish_round(n, carry):
        end_round(n)
        for k in range(4):
            side(n, k).wait_send()
            across(n, k).wait_send()
            last(n, k).wait_send()
        return carry

    lax.fori_loop(0, ROUNDS, finish_round, 0)
    for copy in near_copies() + far_copies():
        copy.wait_send()
    for k in range(1, 4):
        spread_copy(k).wait_send()
        for i in range(2):
            text_copy(i, k).wait_send()

    def finish_out(slot, carry):
        i, step, part, place = placed(slot)

        @pl.when(step == 3)
        def _():
            own_out(i, part, slot).wait()

        @pl.when(step < 3)
        def _():
            out_copy(i, part, slot, place, place).wait()

        return carry

    lax.fori_loop(0, 16, finish_out, 0)


def on_device(
    image,
    modulation,
    query_key_value_weight,
    pooled_down_factor,
    pooled_up_factor,
    request_adapter,
    adapter_slot_table,
    row_request,
    text_key_value,
    query_key_gain,
):
    all_requests = request_adapter.shape[0]
    pool_local, width, rank = pooled_down_factor.shape
    columns = query_key_value_weight.shape[1]
    head_columns = columns // 3
    text_local = text_key_value.shape[1]
    token_local = image.shape[1]
    share = width // 4
    piece_rows = token_local // (2 * ROUNDS)
    held = pltpu.VMEM((2, 4, 2, ROUNDS, piece_rows, head_columns), BF16)

    def dma(*shape):
        return pltpu.SemaphoreType.DMA(shape)

    out, _ = pl.pallas_call(
        block_kernel,
        out_shape=(
            jax.ShapeDtypeStruct((all_requests, 2, ROUNDS, piece_rows, head_columns), BF16),
            jax.ShapeDtypeStruct((2, 4, 2, ROUNDS, piece_rows, width), BF16),
        ),
        in_specs=[ANY, WHOLE, ANY, ANY, ANY, WHOLE, ANY] + [SCALARS] * 3,
        out_specs=(ANY, ANY),
        scratch_shapes=[
            pltpu.VMEM((width, columns), BF16),
            pltpu.VMEM((2, 2, ROUNDS, piece_rows, width), BF16),
            pltpu.VMEM((2, 4, 2, 2, piece_rows, width), BF16),
            held, held, held,
            pltpu.VMEM((2, 4, text_local, 2 * head_columns), BF16),
            pltpu.VMEM((pool_local, rank, columns), BF16),
            pltpu.VMEM((pool_local, rank, share), BF16),
            pltpu.VMEM((2, 2, rank, columns), BF16),
            pltpu.VMEM((2, 2, rank, share), BF16),
            pltpu.VMEM((2, 2, rank, columns), BF16),
            pltpu.VMEM((2, 2, rank, share), BF16),
            pltpu.VMEM((2, rank, columns), BF16),
            pltpu.VMEM((2, rank, share), BF16),
            pltpu.VMEM((2, rank, columns), BF16),
            pltpu.VMEM((2, rank, share), BF16),
            pltpu.VMEM((4, 2, rank, share), BF16),
            pltpu.VMEM((2, rank, width), BF16),
            dma(ROUNDS), dma(), dma(2), dma(2),
        ]
        + [dma(ROUNDS, 4)] * 8
        + [dma(4)] * 2 + [dma(2)] * 2 + [dma(4)] * 2
        + [dma(2, 4)] * 2 + [dma(16)] * 2,
        compiler_params=pltpu.CompilerParams(
            collective_id=0, has_side_effects=True, vmem_limit_bytes=58 * 2**20
        ),
        name="block",
    )(
        image.reshape(2, 2, ROUNDS, piece_rows, width),
        modulation,
        query_key_value_weight,
        jnp.transpose(pooled_down_factor, (0, 2, 1)),
        pooled_up_factor,
        query_key_gain,
        text_key_value.reshape(2, 4, text_local, 2 * head_columns),
        request_adapter,
        adapter_slot_table,
        row_request,
    )
    return out.reshape(all_requests, token_local, head_columns)


def solution(mesh):
    in_specs = (
        P(("groups", "adapt"), "seq", None),
        P(("groups", "adapt"), None, None),
        P(None, "adapt"),
        P("seq", None, None),
        P("seq", None, "adapt"),
        P("groups"),
        P(),
        P("groups"),
        P("groups", "seq", None, "adapt"),
        P(),
    )
    out_specs = P("groups", "seq", "adapt")
    def chosen(*operands):
        image, request_adapter = operands[0], operands[5]
        fits = (
            mesh.shape["seq"] == 4
            and mesh.shape["adapt"] == 4
            and request_adapter.shape[0] == 8
            and image.shape[0] == 2
            and operands[2].shape[1] % (6 * HEAD_SIZE) == 0
            and image.shape[1] % 256 == 0
            and image.shape[2] % 512 == 0
        )
        return (on_device if fits else general_device)(*operands)

    return jax.shard_map(
        chosen, mesh=mesh, in_specs=in_specs, out_specs=out_specs, check_vma=False
    )
```

```python
import functools
import math

import jax
import jax.numpy as jnp
from jax import lax
from jax.experimental import pallas as pl
from jax.experimental.pallas import tpu as pltpu
from jax.sharding import PartitionSpec as P

HEAD_SIZE = 128


def layer_modulate(image, modulation):
    widened = image.astype(jnp.float32)
    centre = widened - jnp.mean(widened, axis=-1, keepdims=True)
    variance = jnp.mean(centre * centre, axis=-1, keepdims=True)
    normed = centre * lax.rsqrt(variance + 1e-06)
    return ((1.0 + modulation[:, 1, None, :]) * normed + modulation[:, 0, None, :]).astype(
        jnp.bfloat16
    )


def rms_scale(values, gain):
    return values * lax.rsqrt(jnp.mean(values * values, axis=-1, keepdims=True) + 1e-06) * gain


def attend_item(operands):
    queries, joined = operands
    key_rows = joined[:, 0]
    value_rows = joined[:, 1]
    query_count = queries.shape[0]
    block = math.gcd(query_count, 512)
    inverse = 1.0 / math.sqrt(queries.shape[-1])
    blocked = queries.reshape(query_count // block, block, queries.shape[-1])

    def one_block(block_rows):
        scores = (
            lax.dot_general(
                block_rows, key_rows, (((1,), (1,)), ((), ())), preferred_element_type=jnp.float32
            )
            * inverse
        )
        highest = jnp.max(scores, axis=-1, keepdims=True)
        weights = jnp.exp(scores - highest)
        weights = weights / jnp.sum(weights, axis=-1, keepdims=True)
        return jnp.dot(
            weights.astype(jnp.bfloat16), value_rows, preferred_element_type=jnp.float32
        ).astype(jnp.bfloat16)

    return lax.map(one_block, blocked).reshape(queries.shape)


def general_device(
    image,
    modulation,
    query_key_value_weight,
    pooled_down_factor,
    pooled_up_factor,
    request_adapter,
    adapter_slot_table,
    row_request,
    text_key_value,
    query_key_gain,
):
    seq_index = lax.axis_index("seq")
    all_requests = request_adapter.shape[0]
    local_pool_slice = pooled_down_factor.shape[0]
    pool_total = adapter_slot_table.shape[0]
    heads_local = query_key_value_weight.shape[1] // (3 * HEAD_SIZE)
    text_local = text_key_value.shape[1]
    modulated = layer_modulate(image, modulation)
    request_match = row_request[:, None] == jnp.arange(all_requests, dtype=jnp.int32)[None, :]
    chosen_ids = jnp.sum(jnp.where(request_match, request_adapter[None, :], 0), axis=1)
    slot_match = chosen_ids[:, None] == jnp.arange(pool_total, dtype=jnp.int32)[None, :]
    slots = jnp.sum(jnp.where(slot_match, adapter_slot_table[None, :], 0), axis=1)
    owned = slots // local_pool_slice == seq_index
    local_match = (slots % local_pool_slice)[:, None] == jnp.arange(
        local_pool_slice, dtype=jnp.int32
    )[None, :]
    slot_picker = (owned[:, None] & local_match).astype(jnp.bfloat16)
    up_terms = jnp.einsum(
        "eq,qfx->efx", slot_picker, pooled_up_factor, preferred_element_type=jnp.float32
    ).astype(jnp.bfloat16)
    down_terms = jnp.einsum(
        "mv,vna->mna", slot_picker, pooled_down_factor, preferred_element_type=jnp.float32
    ).astype(jnp.bfloat16)
    down_fetched, up_fetched = (
        lax.psum(down_terms, "seq").astype(jnp.float32),
        lax.psum(up_terms, "seq").astype(jnp.float32),
    )
    down_fetched = down_fetched.astype(jnp.bfloat16)
    up_fetched = up_fetched.astype(jnp.bfloat16)
    block_rows = lax.all_gather(modulated, "adapt", axis=0, tiled=True)
    shrunk = jnp.einsum(
        "rtd,rdk->rtk", block_rows, down_fetched, preferred_element_type=jnp.float32
    ).astype(jnp.bfloat16)
    frozen = jnp.einsum(
        "rtd,dc->rtc", block_rows, query_key_value_weight, preferred_element_type=jnp.float32
    )
    qkv = frozen + jnp.einsum(
        "rtk,rkc->rtc", shrunk, up_fetched, preferred_element_type=jnp.float32
    )
    token_local = qkv.shape[1]
    qkv = qkv.reshape(all_requests, token_local, heads_local, 3, HEAD_SIZE)
    queries = rms_scale(qkv[:, :, :, 0], query_key_gain[0]).astype(jnp.bfloat16)
    image_keys = rms_scale(qkv[:, :, :, 1], query_key_gain[1]).astype(jnp.bfloat16)
    image_values = qkv[:, :, :, 2].astype(jnp.bfloat16)
    image_pairs = jnp.transpose(jnp.stack([image_keys, image_values], axis=3), (0, 2, 1, 3, 4))
    text_pairs = jnp.transpose(
        text_key_value.reshape(all_requests, text_local, 2, heads_local, HEAD_SIZE), (0, 3, 1, 2, 4)
    )
    joined = jnp.concatenate([image_pairs, text_pairs], axis=2)
    joined = joined.reshape(all_requests * heads_local, token_local + text_local, 2, HEAD_SIZE)
    queries = jnp.transpose(queries, (0, 2, 1, 3)).reshape(
        all_requests * heads_local, token_local, HEAD_SIZE
    )
    query_items, joined_items = (
        lax.all_to_all(queries, "seq", split_axis=0, concat_axis=1, tiled=True),
        lax.all_to_all(joined, "seq", split_axis=0, concat_axis=1, tiled=True),
    )
    attended = lax.map(attend_item, (query_items, joined_items))
    returned = lax.all_to_all(attended, "seq", split_axis=1, concat_axis=0, tiled=True)
    returned = returned.reshape(all_requests, heads_local, token_local, HEAD_SIZE)
    return jnp.transpose(returned, (0, 2, 1, 3)).reshape(
        all_requests, token_local, heads_local * HEAD_SIZE
    )


BF16 = jnp.bfloat16
ROUNDS = 8
EARLY = 4
FIRST = 1
LAG = 4
F32 = jnp.float32
ANY = pl.BlockSpec(memory_space=pl.ANY)
WHOLE = pl.BlockSpec(memory_space=pltpu.VMEM)
SCALARS = pl.BlockSpec(memory_space=pltpu.SMEM)


def flipped(index, k):
    low = 1 - 2 * lax.rem(index, 2) if k % 2 else 0
    high = 2 - 4 * (index // 2) if k // 2 else 0
    return index + low + high


def block_kernel(
    image, modulation, weight, down_pool, up_pool, gain, text, adapter_of, slot_of, request_of,
    out, tok,
    weight_held, mod, rows_held, q_held, k_held, v_held, txt,
    up, down, up_out, down_out, up_near, down_near, up_sent, down_sent, up_far, down_far, down_all, down_whole,
    image_sem, weight_sem, load_sem, pool_sem,
    tok_send, tok_recv, side_send, side_recv, across_send, across_recv, last_send, last_recv,
    near_send, near_recv, far_send, far_recv, spread_send, spread_recv,
    text_send, text_recv, out_send, out_recv,
):
    s = lax.axis_index("seq")
    a = lax.axis_index("adapt")
    x = a // 2
    c = lax.rem(a, 2)
    me = s * 4 + a
    sibling = {"seq": s, "adapt": 2 * x + 1 - c}
    partner = {"seq": s, "adapt": 2 * (1 - x) + c}
    request_row = (x, 1 - x)
    piece_rows = tok.shape[4]
    width = tok.shape[5]
    chunk_rows = 16 * piece_rows
    head_columns = q_held.shape[5]
    heads = head_columns // HEAD_SIZE
    token_local = 2 * ROUNDS * piece_rows
    half_rows = ROUNDS * piece_rows
    text_rows = 4 * txt.shape[2]

    def remote(source, target, send, recv, device):
        return pltpu.make_async_remote_copy(
            src_ref=source, dst_ref=target, send_sem=send, recv_sem=recv,
            device_id=device, device_id_type=pl.DeviceIdType.MESH,
        )

    weight_copy = pltpu.make_async_copy(weight, weight_held, weight_sem)

    def image_copy(n):
        return pltpu.make_async_copy(image.at[:, :, n], mod.at[:, :, n], image_sem.at[n])

    for n in range(ROUNDS):
        image_copy(n).start()
    share = down_all.shape[3]
    quarter = pl.ds(pl.multiple_of(a * share, HEAD_SIZE), share)
    pool_copies = (
        pltpu.make_async_copy(down_pool.at[:, :, quarter], down, pool_sem.at[0]),
        pltpu.make_async_copy(up_pool, up, pool_sem.at[1]),
    )
    for copy in pool_copies:
        copy.start()
    weight_copy.start()

    barrier = pltpu.get_barrier_semaphore()
    for k in range(1, 16):
        other = lax.rem(me + k, 16)
        pl.semaphore_signal(
            barrier, inc=1, device_id={"seq": other // 4, "adapt": lax.rem(other, 4)},
            device_id_type=pl.DeviceIdType.MESH,
        )
    pl.semaphore_wait(barrier, 15)

    pool_local = up.shape[0]

    def picked(pool, place):
        terms = []
        for r in range(2):
            slot = slot_of[adapter_of[request_of[4 * r + place]]]
            mine = jnp.where(slot // pool_local == s, 1.0, 0.0)
            terms.append((pool[lax.rem(slot, pool_local)].astype(F32) * mine).astype(BF16))
        return terms

    def near_copies():
        to = {"seq": flipped(s, 1), "adapt": a}
        copies = []
        for n in range(2):
            copies.append(remote(up_out.at[n], up_near.at[n], near_send.at[n], near_recv.at[n], to))
            copies.append(
                remote(down_out.at[n], down_near.at[n], near_send.at[2 + n], near_recv.at[2 + n], to)
            )
        return copies

    def far_copies():
        to = {"seq": flipped(s, 2), "adapt": a}
        return [
            remote(up_sent, up_far, far_send.at[0], far_recv.at[0], to),
            remote(down_sent, down_far, far_send.at[1], far_recv.at[1], to),
        ]

    def spread_copy(k):
        return remote(
            down_all.at[a], down_all.at[a], spread_send.at[k], spread_recv.at[k],
            {"seq": s, "adapt": flipped(a, k)},
        )

    def spread_in(k):
        other = flipped(a, k)
        return remote(
            down_all.at[other], down_all.at[other], spread_send.at[k], spread_recv.at[k], sibling
        )

    def handed(n, j, h):
        place = 2 * c + j
        mine = jnp.logical_and(place == s, c == h)
        recv = tok_recv.at[n, s]
        source, target = mod.at[j, h, n], tok.at[0, s, h, n]
        away = remote(
            source, target, tok_send.at[n, 2 * j + h], recv, {"seq": place, "adapt": 2 * x + h}
        )
        return mine, away, pltpu.make_async_copy(source, target, recv)

    def start_round(n):
        for j in range(2):
            for h in range(2):
                mine, away, here = handed(n, j, h)

                @pl.when(mine)
                def _():
                    here.start()

                @pl.when(jnp.logical_not(mine))
                def _():
                    away.start()

    def end_round(n):
        for j in range(2):
            for h in range(2):
                mine, away, _ = handed(n, j, h)

                @pl.when(jnp.logical_not(mine))
                def _():
                    away.wait_send()

    def modulate_round(n):
        image_copy(n).wait()
        step_rows = 16
        parts = piece_rows // step_rows

        def one(b, carry):
            j = b // (2 * parts)
            h = lax.rem(b // parts, 2)
            rows = pl.ds(pl.multiple_of(lax.rem(b, parts) * step_rows, step_rows), step_rows)
            widened = mod[j, h, n, rows, :].astype(F32)
            centre = widened - jnp.mean(widened, axis=-1, keepdims=True)
            variance = jnp.mean(centre * centre, axis=-1, keepdims=True)
            normed = centre * lax.rsqrt(variance + 1e-06)
            shift = modulation[j, 0:1, :]
            scale = modulation[j, 1:2, :]
            mod[j, h, n, rows, :] = ((1.0 + scale) * normed + shift).astype(BF16)
            return carry

        lax.fori_loop(0, 4 * parts, one, 0)

    def piece(i, n, k, core):
        return tok.at[i, flipped(s, k), core, n]

    def first(n, k):
        here = piece(0, n, k, c)
        return remote(here, here, tok_send.at[n, 0], tok_recv.at[n, flipped(s, k)], sibling)

    def side(n, k):
        here = piece(0, n, k, c)
        return remote(here, here, side_send.at[n, k], side_recv.at[n, k], sibling)

    def side_in(n, k):
        there = piece(0, n, k, 1 - c)
        return remote(there, there, side_send.at[n, k], side_recv.at[n, k], sibling)

    def across(n, k):
        return remote(
            piece(0, n, k, c), piece(1, n, k, c), across_send.at[n, k], across_recv.at[n, k], partner
        )

    def last(n, k):
        here = piece(1, n, k, c)
        return remote(here, here, last_send.at[n, k], last_recv.at[n, k], sibling)

    def last_in(n, k):
        there = piece(1, n, k, 1 - c)
        return remote(there, there, last_send.at[n, k], last_recv.at[n, k], sibling)

    def text_copy(i, k):
        place = flipped(s, k)
        row = request_row[i]
        return remote(
            text.at[row, place], txt.at[i, s], text_send.at[i, k], text_recv.at[i, k],
            {"seq": place, "adapt": a},
        )

    def text_in(i, k):
        place = flipped(s, k)
        return remote(
            txt.at[i, place], txt.at[i, place], text_send.at[i, k], text_recv.at[i, k], sibling
        )

    def own_text(i):
        return pltpu.make_async_copy(text.at[request_row[i], s], txt.at[i, s], text_recv.at[i, 0])

    for i in range(2):
        own_text(i).start()

    def opening(n, carry):
        modulate_round(n)

        @pl.when(n < EARLY)
        def _():
            start_round(n)

        @pl.when(n == FIRST - 1)
        def _():
            for copy in pool_copies:
                copy.wait()
            for m, k in enumerate((1, 3)):
                place = flipped(s, k)
                for r, (one, two) in enumerate(zip(picked(up, place), picked(down, place))):
                    up_out[m, r] = one
                    down_out[m, r] = two
            for copy in near_copies():
                copy.start()

        return carry

    lax.fori_loop(0, ROUNDS, opening, 0)

    def pass_on(n, sources=(1, 2, 3)):
        for k in sources:
            first(n, k).wait_recv()
            across(n, k).start()
            side(n, k).start()

    def pass_own(n, carry):
        pass_on(n, (0,))
        return carry

    lax.fori_loop(0, EARLY, pass_own, 0)

    for copy in near_copies():
        copy.wait_recv()
    away = flipped(s, 2)
    for r, (one, two) in enumerate(zip(picked(up, away), picked(down, away))):
        up_sent[r] = one + up_near[1, r]
        down_sent[r] = two + down_near[1, r]
    for copy in far_copies():
        copy.start()
    for r, (one, two) in enumerate(zip(picked(up, s), picked(down, s))):
        up_near[0, r] = one + up_near[0, r]
        down_near[0, r] = two + down_near[0, r]

    def start_rest(n, carry):
        start_round(n)
        return carry

    lax.fori_loop(EARLY, ROUNDS, start_rest, 0)
    for i in range(2):
        for k in (2, 3, 1):
            text_copy(i, k).start()
    lax.fori_loop(EARLY, ROUNDS, pass_own, 0)

    def load(i, n):
        return pltpu.make_async_copy(
            tok.at[i, :, :, pl.ds(2 * n, 2)], rows_held.at[i], load_sem.at[i]
        )

    def project(i, n):
        rows = rows_held[i].reshape(chunk_rows, width)
        row = request_row[i]
        shrunk = lax.dot_general(
            rows, down_whole[row], (((1,), (1,)), ((), ())), preferred_element_type=F32
        ).astype(BF16)
        wide = 6 * HEAD_SIZE
        for part in range(weight_held.shape[1] // wide):
            columns = slice(part * wide, (part + 1) * wide)
            qkv = jnp.dot(rows, weight_held[:, columns], preferred_element_type=F32)
            qkv = qkv + jnp.dot(shrunk, up_far[row, :, columns], preferred_element_type=F32)
            for h in range(2):
                head = slice((2 * part + h) * HEAD_SIZE, (2 * part + h + 1) * HEAD_SIZE)
                q, k, v = (
                    qkv[:, (3 * h + m) * HEAD_SIZE : (3 * h + m + 1) * HEAD_SIZE] for m in range(3)
                )
                shape = (4, 2, 2, piece_rows, HEAD_SIZE)
                pair = pl.ds(2 * n, 2)
                q_held[i, :, :, pair, :, head] = rms_scale(q, gain[0:1, :]).astype(BF16).reshape(shape)
                k_held[i, :, :, pair, :, head] = rms_scale(k, gain[1:2, :]).astype(BF16).reshape(shape)
                v_held[i, :, :, pair, :, head] = v.astype(BF16).reshape(shape)

    def hand_over(n):
        for k in range(4):
            across(n, k).wait_recv()
            last(n, k).start()

    def lead(n, carry):
        pass_on(n)

        @pl.when(n > 1)
        def _():
            hand_over(n - 2)

        return carry

    lax.fori_loop(0, LAG, lead, 0)
    for copy in far_copies():
        copy.wait_recv()
    up_far[...] = up_near[0] + up_far[...]
    down_all[a] = down_near[0] + down_far[...]
    for k in range(1, 4):
        spread_copy(k).start()
    weight_copy.wait()

    def stage(n, carry):
        pass_on(n)

        @pl.when(n == LAG)
        def _():
            for k in range(1, 4):
                spread_in(k).wait_recv()
            for k in range(4):
                down_whole[:, :, k * share : (k + 1) * share] = down_all[k]

        hand_over(n - 2)
        for m in range(2):
            for k in range(4):
                side_in(2 * (n - LAG) + m, k).wait_recv()
        load(0, n - LAG).start()

        @pl.when(n > LAG)
        def _():
            for m in range(2):
                for k in range(4):
                    last_in(2 * (n - LAG - 1) + m, k).wait_recv()
            load(1, n - LAG - 1).start()

        load(0, n - LAG).wait()
        project(0, n - LAG)

        @pl.when(n > LAG)
        def _():
            load(1, n - LAG - 1).wait()
            project(1, n - LAG - 1)

        return carry

    lax.fori_loop(LAG, ROUNDS, stage, 0)

    factor = math.log2(math.e) / math.sqrt(HEAD_SIZE)

    def target(step):
        return jnp.where(
            step == 3, s,
            jnp.where(step == 2, flipped(s, 1), jnp.where(step == 1, flipped(s, 3), flipped(s, 2))),
        )

    def out_copy(i, part, slot, row_from, place):
        row = 4 * jnp.where(i == 0, x, 1 - x) + row_from
        return remote(
            q_held.at[i, place, part], out.at[row, part], out_send.at[slot], out_recv.at[slot],
            {"seq": place, "adapt": a},
        )

    def own_out(i, part, slot):
        row = 4 * jnp.where(i == 0, x, 1 - x) + s
        return pltpu.make_async_copy(q_held.at[i, s, part], out.at[row, part], out_recv.at[slot])

    def placed(slot):
        far = slot < 8
        i = jnp.where(far, slot // 4, lax.rem(slot // 2, 2))
        step = jnp.where(far, lax.rem(slot // 2, 2), slot // 4)
        return i, step, lax.rem(slot, 2), target(step)

    def attend_step(slot, carry):
        i, step, part, place = placed(slot)

        @pl.when(slot == 2)
        def _():
            hand_over(ROUNDS - 2)
            hand_over(ROUNDS - 1)

        @pl.when(slot == 4)
        def _():
            pair = ROUNDS // 2 - 1
            for m in range(2):
                for k in range(4):
                    last_in(2 * pair + m, k).wait_recv()
            load(1, pair).start()
            load(1, pair).wait()
            project(1, pair)

        for r in range(2):
            @pl.when(slot == 4 * r)
            def _():
                own_text(r).wait()
                for k in range(1, 4):
                    text_in(r, k).wait_recv()

        def scores(h):
            head = slice(h * HEAD_SIZE, (h + 1) * HEAD_SIZE)
            query = q_held[i, place, part, :, :, head].reshape(half_rows, HEAD_SIZE)
            image_keys = k_held[i, :, :, :, :, head].reshape(4 * token_local, HEAD_SIZE)
            text_keys = txt[i, :, :, head].reshape(text_rows, HEAD_SIZE)
            return tuple(
                lax.dot_general(
                    query, key_rows, (((1,), (1,)), ((), ())), preferred_element_type=F32
                )
                for key_rows in (image_keys, text_keys)
            )

        ready = scores(0)
        for h in range(heads):
            one, two = ready
            if h + 1 < heads:
                ready = scores(h + 1)
            head = slice(h * HEAD_SIZE, (h + 1) * HEAD_SIZE)
            value_head = slice(head_columns + h * HEAD_SIZE, head_columns + (h + 1) * HEAD_SIZE)
            highest = jnp.maximum(
                jnp.max(one, axis=-1, keepdims=True), jnp.max(two, axis=-1, keepdims=True)
            )
            one = jnp.exp2((one - highest) * factor)
            two = jnp.exp2((two - highest) * factor)
            share = 1.0 / (jnp.sum(one, axis=-1, keepdims=True) + jnp.sum(two, axis=-1, keepdims=True))
            image_values = v_held[i, :, :, :, :, head].reshape(4 * token_local, HEAD_SIZE)
            text_values = txt[i, :, :, value_head].reshape(text_rows, HEAD_SIZE)
            total = jnp.dot((one * share).astype(BF16), image_values, preferred_element_type=F32)
            total = total + jnp.dot(
                (two * share).astype(BF16), text_values, preferred_element_type=F32
            )
            q_held[i, place, part, :, :, head] = total.astype(BF16).reshape(
                ROUNDS, piece_rows, HEAD_SIZE
            )

        @pl.when(step == 3)
        def _():
            own_out(i, part, slot).start()

        @pl.when(step < 3)
        def _():
            out_copy(i, part, slot, s, place).start()

        return carry

    lax.fori_loop(0, 16, attend_step, 0)

    def finish_round(n, carry):
        end_round(n)
        for k in range(4):
            side(n, k).wait_send()
            across(n, k).wait_send()
            last(n, k).wait_send()
        return carry

    lax.fori_loop(0, ROUNDS, finish_round, 0)
    for copy in near_copies() + far_copies():
        copy.wait_send()
    for k in range(1, 4):
        spread_copy(k).wait_send()
        for i in range(2):
            text_copy(i, k).wait_send()

    def finish_out(slot, carry):
        i, step, part, place = placed(slot)

        @pl.when(step == 3)
        def _():
            own_out(i, part, slot).wait()

        @pl.when(step < 3)
        def _():
            out_copy(i, part, slot, place, place).wait()

        return carry

    lax.fori_loop(0, 16, finish_out, 0)


def on_device(
    image,
    modulation,
    query_key_value_weight,
    pooled_down_factor,
    pooled_up_factor,
    request_adapter,
    adapter_slot_table,
    row_request,
    text_key_value,
    query_key_gain,
):
    all_requests = request_adapter.shape[0]
    pool_local, width, rank = pooled_down_factor.shape
    columns = query_key_value_weight.shape[1]
    head_columns = columns // 3
    text_local = text_key_value.shape[1]
    token_local = image.shape[1]
    share = width // 4
    piece_rows = token_local // (2 * ROUNDS)
    held = pltpu.VMEM((2, 4, 2, ROUNDS, piece_rows, head_columns), BF16)

    def dma(*shape):
        return pltpu.SemaphoreType.DMA(shape)

    out, _ = pl.pallas_call(
        block_kernel,
        out_shape=(
            jax.ShapeDtypeStruct((all_requests, 2, ROUNDS, piece_rows, head_columns), BF16),
            jax.ShapeDtypeStruct((2, 4, 2, ROUNDS, piece_rows, width), BF16),
        ),
        in_specs=[ANY, WHOLE, ANY, ANY, ANY, WHOLE, ANY] + [SCALARS] * 3,
        out_specs=(ANY, ANY),
        scratch_shapes=[
            pltpu.VMEM((width, columns), BF16),
            pltpu.VMEM((2, 2, ROUNDS, piece_rows, width), BF16),
            pltpu.VMEM((2, 4, 2, 2, piece_rows, width), BF16),
            held, held, held,
            pltpu.VMEM((2, 4, text_local, 2 * head_columns), BF16),
            pltpu.VMEM((pool_local, rank, columns), BF16),
            pltpu.VMEM((pool_local, rank, share), BF16),
            pltpu.VMEM((2, 2, rank, columns), BF16),
            pltpu.VMEM((2, 2, rank, share), BF16),
            pltpu.VMEM((2, 2, rank, columns), BF16),
            pltpu.VMEM((2, 2, rank, share), BF16),
            pltpu.VMEM((2, rank, columns), BF16),
            pltpu.VMEM((2, rank, share), BF16),
            pltpu.VMEM((2, rank, columns), BF16),
            pltpu.VMEM((2, rank, share), BF16),
            pltpu.VMEM((4, 2, rank, share), BF16),
            pltpu.VMEM((2, rank, width), BF16),
            dma(ROUNDS), dma(), dma(2), dma(2),
        ]
        + [dma(ROUNDS, 4)] * 8
        + [dma(4)] * 2 + [dma(2)] * 2 + [dma(4)] * 2
        + [dma(2, 4)] * 2 + [dma(16)] * 2,
        compiler_params=pltpu.CompilerParams(
            collective_id=0, has_side_effects=True, vmem_limit_bytes=58 * 2**20
        ),
        name="block",
    )(
        image.reshape(2, 2, ROUNDS, piece_rows, width),
        modulation,
        query_key_value_weight,
        jnp.transpose(pooled_down_factor, (0, 2, 1)),
        pooled_up_factor,
        query_key_gain,
        text_key_value.reshape(2, 4, text_local, 2 * head_columns),
        request_adapter,
        adapter_slot_table,
        row_request,
    )
    return out.reshape(all_requests, token_local, head_columns)


def solution(mesh):
    in_specs = (
        P(("groups", "adapt"), "seq", None),
        P(("groups", "adapt"), None, None),
        P(None, "adapt"),
        P("seq", None, None),
        P("seq", None, "adapt"),
        P("groups"),
        P(),
        P("groups"),
        P("groups", "seq", None, "adapt"),
        P(),
    )
    out_specs = P("groups", "seq", "adapt")
    def chosen(*operands):
        image, request_adapter = operands[0], operands[5]
        fits = (
            mesh.shape["seq"] == 4
            and mesh.shape["adapt"] == 4
            and request_adapter.shape[0] == 8
            and image.shape[0] == 2
            and operands[2].shape[1] % (6 * HEAD_SIZE) == 0
            and image.shape[1] % 256 == 0
            and image.shape[2] % 512 == 0
        )
        return (on_device if fits else general_device)(*operands)

    return jax.shard_map(
        chosen, mesh=mesh, in_specs=in_specs, out_specs=out_specs, check_vma=False
    )
```

```python
import functools
import math

import jax
import jax.numpy as jnp
from jax import lax
from jax.experimental import pallas as pl
from jax.experimental.pallas import tpu as pltpu
from jax.sharding import PartitionSpec as P

HEAD_SIZE = 128


def layer_modulate(image, modulation):
    widened = image.astype(jnp.float32)
    centre = widened - jnp.mean(widened, axis=-1, keepdims=True)
    variance = jnp.mean(centre * centre, axis=-1, keepdims=True)
    normed = centre * lax.rsqrt(variance + 1e-06)
    return ((1.0 + modulation[:, 1, None, :]) * normed + modulation[:, 0, None, :]).astype(
        jnp.bfloat16
    )


def rms_scale(values, gain):
    return values * lax.rsqrt(jnp.mean(values * values, axis=-1, keepdims=True) + 1e-06) * gain


def attend_item(operands):
    queries, joined = operands
    key_rows = joined[:, 0]
    value_rows = joined[:, 1]
    query_count = queries.shape[0]
    block = math.gcd(query_count, 512)
    inverse = 1.0 / math.sqrt(queries.shape[-1])
    blocked = queries.reshape(query_count // block, block, queries.shape[-1])

    def one_block(block_rows):
        scores = (
            lax.dot_general(
                block_rows, key_rows, (((1,), (1,)), ((), ())), preferred_element_type=jnp.float32
            )
            * inverse
        )
        highest = jnp.max(scores, axis=-1, keepdims=True)
        weights = jnp.exp(scores - highest)
        weights = weights / jnp.sum(weights, axis=-1, keepdims=True)
        return jnp.dot(
            weights.astype(jnp.bfloat16), value_rows, preferred_element_type=jnp.float32
        ).astype(jnp.bfloat16)

    return lax.map(one_block, blocked).reshape(queries.shape)


def general_device(
    image,
    modulation,
    query_key_value_weight,
    pooled_down_factor,
    pooled_up_factor,
    request_adapter,
    adapter_slot_table,
    row_request,
    text_key_value,
    query_key_gain,
):
    seq_index = lax.axis_index("seq")
    all_requests = request_adapter.shape[0]
    local_pool_slice = pooled_down_factor.shape[0]
    pool_total = adapter_slot_table.shape[0]
    heads_local = query_key_value_weight.shape[1] // (3 * HEAD_SIZE)
    text_local = text_key_value.shape[1]
    modulated = layer_modulate(image, modulation)
    request_match = row_request[:, None] == jnp.arange(all_requests, dtype=jnp.int32)[None, :]
    chosen_ids = jnp.sum(jnp.where(request_match, request_adapter[None, :], 0), axis=1)
    slot_match = chosen_ids[:, None] == jnp.arange(pool_total, dtype=jnp.int32)[None, :]
    slots = jnp.sum(jnp.where(slot_match, adapter_slot_table[None, :], 0), axis=1)
    owned = slots // local_pool_slice == seq_index
    local_match = (slots % local_pool_slice)[:, None] == jnp.arange(
        local_pool_slice, dtype=jnp.int32
    )[None, :]
    slot_picker = (owned[:, None] & local_match).astype(jnp.bfloat16)
    up_terms = jnp.einsum(
        "eq,qfx->efx", slot_picker, pooled_up_factor, preferred_element_type=jnp.float32
    ).astype(jnp.bfloat16)
    down_terms = jnp.einsum(
        "mv,vna->mna", slot_picker, pooled_down_factor, preferred_element_type=jnp.float32
    ).astype(jnp.bfloat16)
    down_fetched, up_fetched = (
        lax.psum(down_terms, "seq").astype(jnp.float32),
        lax.psum(up_terms, "seq").astype(jnp.float32),
    )
    down_fetched = down_fetched.astype(jnp.bfloat16)
    up_fetched = up_fetched.astype(jnp.bfloat16)
    block_rows = lax.all_gather(modulated, "adapt", axis=0, tiled=True)
    shrunk = jnp.einsum(
        "rtd,rdk->rtk", block_rows, down_fetched, preferred_element_type=jnp.float32
    ).astype(jnp.bfloat16)
    frozen = jnp.einsum(
        "rtd,dc->rtc", block_rows, query_key_value_weight, preferred_element_type=jnp.float32
    )
    qkv = frozen + jnp.einsum(
        "rtk,rkc->rtc", shrunk, up_fetched, preferred_element_type=jnp.float32
    )
    token_local = qkv.shape[1]
    qkv = qkv.reshape(all_requests, token_local, heads_local, 3, HEAD_SIZE)
    queries = rms_scale(qkv[:, :, :, 0], query_key_gain[0]).astype(jnp.bfloat16)
    image_keys = rms_scale(qkv[:, :, :, 1], query_key_gain[1]).astype(jnp.bfloat16)
    image_values = qkv[:, :, :, 2].astype(jnp.bfloat16)
    image_pairs = jnp.transpose(jnp.stack([image_keys, image_values], axis=3), (0, 2, 1, 3, 4))
    text_pairs = jnp.transpose(
        text_key_value.reshape(all_requests, text_local, 2, heads_local, HEAD_SIZE), (0, 3, 1, 2, 4)
    )
    joined = jnp.concatenate([image_pairs, text_pairs], axis=2)
    joined = joined.reshape(all_requests * heads_local, token_local + text_local, 2, HEAD_SIZE)
    queries = jnp.transpose(queries, (0, 2, 1, 3)).reshape(
        all_requests * heads_local, token_local, HEAD_SIZE
    )
    query_items, joined_items = (
        lax.all_to_all(queries, "seq", split_axis=0, concat_axis=1, tiled=True),
        lax.all_to_all(joined, "seq", split_axis=0, concat_axis=1, tiled=True),
    )
    attended = lax.map(attend_item, (query_items, joined_items))
    returned = lax.all_to_all(attended, "seq", split_axis=1, concat_axis=0, tiled=True)
    returned = returned.reshape(all_requests, heads_local, token_local, HEAD_SIZE)
    return jnp.transpose(returned, (0, 2, 1, 3)).reshape(
        all_requests, token_local, heads_local * HEAD_SIZE
    )


BF16 = jnp.bfloat16
ROUNDS = 8
EARLY = 4
FIRST = 1
LAG = 4
F32 = jnp.float32
ANY = pl.BlockSpec(memory_space=pl.ANY)
WHOLE = pl.BlockSpec(memory_space=pltpu.VMEM)
SCALARS = pl.BlockSpec(memory_space=pltpu.SMEM)


def flipped(index, k):
    low = 1 - 2 * lax.rem(index, 2) if k % 2 else 0
    high = 2 - 4 * (index // 2) if k // 2 else 0
    return index + low + high


def block_kernel(
    image, modulation, weight, down_pool, up_pool, gain, text, adapter_of, slot_of, request_of,
    out, tok,
    weight_held, mod, rows_held, q_held, k_held, v_held, txt,
    up, down, up_out, down_out, up_near, down_near, up_sent, down_sent, up_far, down_far, down_all, down_whole,
    image_sem, weight_sem, load_sem, pool_sem,
    tok_send, tok_recv, side_send, side_recv, across_send, across_recv, last_send, last_recv,
    near_send, near_recv, far_send, far_recv, spread_send, spread_recv,
    text_send, text_recv, out_send, out_recv,
):
    s = lax.axis_index("seq")
    a = lax.axis_index("adapt")
    x = a // 2
    c = lax.rem(a, 2)
    me = s * 4 + a
    sibling = {"seq": s, "adapt": 2 * x + 1 - c}
    partner = {"seq": s, "adapt": 2 * (1 - x) + c}
    request_row = (x, 1 - x)
    piece_rows = tok.shape[4]
    width = tok.shape[5]
    chunk_rows = 16 * piece_rows
    head_columns = q_held.shape[5]
    heads = head_columns // HEAD_SIZE
    token_local = 2 * ROUNDS * piece_rows
    half_rows = ROUNDS * piece_rows
    text_rows = 4 * txt.shape[2]

    def remote(source, target, send, recv, device):
        return pltpu.make_async_remote_copy(
            src_ref=source, dst_ref=target, send_sem=send, recv_sem=recv,
            device_id=device, device_id_type=pl.DeviceIdType.MESH,
        )

    weight_copy = pltpu.make_async_copy(weight, weight_held, weight_sem)

    def image_copy(n):
        return pltpu.make_async_copy(image.at[:, :, n], mod.at[:, :, n], image_sem.at[n])

    for n in range(ROUNDS):
        image_copy(n).start()
    share = down_all.shape[3]
    quarter = pl.ds(pl.multiple_of(a * share, HEAD_SIZE), share)
    pool_copies = (
        pltpu.make_async_copy(down_pool.at[:, :, quarter], down, pool_sem.at[0]),
        pltpu.make_async_copy(up_pool, up, pool_sem.at[1]),
    )
    for copy in pool_copies:
        copy.start()
    weight_copy.start()

    barrier = pltpu.get_barrier_semaphore()
    for k in range(1, 16):
        other = lax.rem(me + k, 16)
        pl.semaphore_signal(
            barrier, inc=1, device_id={"seq": other // 4, "adapt": lax.rem(other, 4)},
            device_id_type=pl.DeviceIdType.MESH,
        )
    pl.semaphore_wait(barrier, 15)

    pool_local = up.shape[0]

    def picked(pool, place):
        terms = []
        for r in range(2):
            slot = slot_of[adapter_of[request_of[4 * r + place]]]
            mine = jnp.where(slot // pool_local == s, 1.0, 0.0)
            terms.append((pool[lax.rem(slot, pool_local)].astype(F32) * mine).astype(BF16))
        return terms

    def near_copies():
        to = {"seq": flipped(s, 1), "adapt": a}
        copies = []
        for n in range(2):
            copies.append(remote(up_out.at[n], up_near.at[n], near_send.at[n], near_recv.at[n], to))
            copies.append(
                remote(down_out.at[n], down_near.at[n], near_send.at[2 + n], near_recv.at[2 + n], to)
            )
        return copies

    def far_copies():
        to = {"seq": flipped(s, 2), "adapt": a}
        return [
            remote(up_sent, up_far, far_send.at[0], far_recv.at[0], to),
            remote(down_sent, down_far, far_send.at[1], far_recv.at[1], to),
        ]

    def spread_copy(k):
        return remote(
            down_all.at[a], down_all.at[a], spread_send.at[k], spread_recv.at[k],
            {"seq": s, "adapt": flipped(a, k)},
        )

    def spread_in(k):
        other = flipped(a, k)
        return remote(
            down_all.at[other], down_all.at[other], spread_send.at[k], spread_recv.at[k], sibling
        )

    def handed(n, j, h):
        place = 2 * c + j
        mine = jnp.logical_and(place == s, c == h)
        recv = tok_recv.at[n, s]
        source, target = mod.at[j, h, n], tok.at[0, s, h, n]
        away = remote(
            source, target, tok_send.at[n, 2 * j + h], recv, {"seq": place, "adapt": 2 * x + h}
        )
        return mine, away, pltpu.make_async_copy(source, target, recv)

    def start_round(n):
        for j in range(2):
            for h in range(2):
                mine, away, here = handed(n, j, h)

                @pl.when(mine)
                def _():
                    here.start()

                @pl.when(jnp.logical_not(mine))
                def _():
                    away.start()

    def end_round(n):
        for j in range(2):
            for h in range(2):
                mine, away, _ = handed(n, j, h)

                @pl.when(jnp.logical_not(mine))
                def _():
                    away.wait_send()

    def modulate_round(n):
        image_copy(n).wait()
        step_rows = 16
        parts = piece_rows // step_rows

        def one(b, carry):
            j = b // (2 * parts)
            h = lax.rem(b // parts, 2)
            rows = pl.ds(pl.multiple_of(lax.rem(b, parts) * step_rows, step_rows), step_rows)
            widened = mod[j, h, n, rows, :].astype(F32)
            centre = widened - jnp.mean(widened, axis=-1, keepdims=True)
            variance = jnp.mean(centre * centre, axis=-1, keepdims=True)
            normed = centre * lax.rsqrt(variance + 1e-06)
            shift = modulation[j, 0:1, :]
            scale = modulation[j, 1:2, :]
            mod[j, h, n, rows, :] = ((1.0 + scale) * normed + shift).astype(BF16)
            return carry

        lax.fori_loop(0, 4 * parts, one, 0)

    def piece(i, n, k, core):
        return tok.at[i, flipped(s, k), core, n]

    def first(n, k):
        here = piece(0, n, k, c)
        return remote(here, here, tok_send.at[n, 0], tok_recv.at[n, flipped(s, k)], sibling)

    def side(n, k):
        here = piece(0, n, k, c)
        return remote(here, here, side_send.at[n, k], side_recv.at[n, k], sibling)

    def side_in(n, k):
        there = piece(0, n, k, 1 - c)
        return remote(there, there, side_send.at[n, k], side_recv.at[n, k], sibling)

    def across(n, k):
        return remote(
            piece(0, n, k, c), piece(1, n, k, c), across_send.at[n, k], across_recv.at[n, k], partner
        )

    def last(n, k):
        here = piece(1, n, k, c)
        return remote(here, here, last_send.at[n, k], last_recv.at[n, k], sibling)

    def last_in(n, k):
        there = piece(1, n, k, 1 - c)
        return remote(there, there, last_send.at[n, k], last_recv.at[n, k], sibling)

    def text_copy(i, k):
        place = flipped(s, k)
        row = request_row[i]
        return remote(
            text.at[row, place], txt.at[i, s], text_send.at[i, k], text_recv.at[i, k],
            {"seq": place, "adapt": a},
        )

    def text_in(i, k):
        place = flipped(s, k)
        return remote(
            txt.at[i, place], txt.at[i, place], text_send.at[i, k], text_recv.at[i, k], sibling
        )

    def own_text(i):
        return pltpu.make_async_copy(text.at[request_row[i], s], txt.at[i, s], text_recv.at[i, 0])

    for i in range(2):
        own_text(i).start()

    def opening(n, carry):
        modulate_round(n)

        @pl.when(n < EARLY)
        def _():
            start_round(n)

        @pl.when(n == FIRST - 1)
        def _():
            for copy in pool_copies:
                copy.wait()
            for m, k in enumerate((1, 3)):
                place = flipped(s, k)
                for r, (one, two) in enumerate(zip(picked(up, place), picked(down, place))):
                    up_out[m, r] = one
                    down_out[m, r] = two
            for copy in near_copies():
                copy.start()

        return carry

    lax.fori_loop(0, ROUNDS, opening, 0)

    def pass_on(n, sources=(1, 2, 3)):
        for k in sources:
            first(n, k).wait_recv()
            across(n, k).start()
            side(n, k).start()

    def pass_own(n, carry):
        pass_on(n, (0,))
        return carry

    lax.fori_loop(0, EARLY, pass_own, 0)

    for copy in near_copies():
        copy.wait_recv()
    away = flipped(s, 2)
    for r, (one, two) in enumerate(zip(picked(up, away), picked(down, away))):
        up_sent[r] = one + up_near[1, r]
        down_sent[r] = two + down_near[1, r]
    for copy in far_copies():
        copy.start()
    for r, (one, two) in enumerate(zip(picked(up, s), picked(down, s))):
        up_near[0, r] = one + up_near[0, r]
        down_near[0, r] = two + down_near[0, r]

    def start_rest(n, carry):
        start_round(n)
        return carry

    lax.fori_loop(EARLY, ROUNDS, start_rest, 0)
    for i in range(2):
        for k in (2, 3, 1):
            text_copy(i, k).start()
    lax.fori_loop(EARLY, ROUNDS, pass_own, 0)

    def load(i, n):
        return pltpu.make_async_copy(
            tok.at[i, :, :, pl.ds(2 * n, 2)], rows_held.at[i], load_sem.at[i]
        )

    def project(i, n):
        rows = rows_held[i].reshape(chunk_rows, width)
        row = request_row[i]
        shrunk = lax.dot_general(
            rows, down_whole[row], (((1,), (1,)), ((), ())), preferred_element_type=F32
        ).astype(BF16)
        wide = 6 * HEAD_SIZE
        for part in range(weight_held.shape[1] // wide):
            columns = slice(part * wide, (part + 1) * wide)
            qkv = jnp.dot(rows, weight_held[:, columns], preferred_element_type=F32)
            qkv = qkv + jnp.dot(shrunk, up_far[row, :, columns], preferred_element_type=F32)
            for h in range(2):
                head = slice((2 * part + h) * HEAD_SIZE, (2 * part + h + 1) * HEAD_SIZE)
                q, k, v = (
                    qkv[:, (3 * h + m) * HEAD_SIZE : (3 * h + m + 1) * HEAD_SIZE] for m in range(3)
                )
                shape = (4, 2, 2, piece_rows, HEAD_SIZE)
                pair = pl.ds(2 * n, 2)
                q_held[i, :, :, pair, :, head] = rms_scale(q, gain[0:1, :]).astype(BF16).reshape(shape)
                k_held[i, :, :, pair, :, head] = rms_scale(k, gain[1:2, :]).astype(BF16).reshape(shape)
                v_held[i, :, :, pair, :, head] = v.astype(BF16).reshape(shape)

    def hand_over(n):
        for k in range(4):
            across(n, k).wait_recv()
            last(n, k).start()

    def lead(n, carry):
        pass_on(n)

        @pl.when(n > 1)
        def _():
            hand_over(n - 2)

        return carry

    lax.fori_loop(0, LAG, lead, 0)
    for copy in far_copies():
        copy.wait_recv()
    up_far[...] = up_near[0] + up_far[...]
    down_all[a] = down_near[0] + down_far[...]
    for k in range(1, 4):
        spread_copy(k).start()
    weight_copy.wait()

    def project_late(pair, carry):
        for m in range(2):
            for k in range(4):
                last_in(2 * pair + m, k).wait_recv()
        load(1, pair).start()
        load(1, pair).wait()
        project(1, pair)
        return carry

    def stage(n, carry):
        pass_on(n)

        @pl.when(n == LAG)
        def _():
            for k in range(1, 4):
                spread_in(k).wait_recv()
            for k in range(4):
                down_whole[:, :, k * share : (k + 1) * share] = down_all[k]

        for m in range(2):
            for k in range(4):
                side_in(2 * (n - LAG) + m, k).wait_recv()
        load(0, n - LAG).start()
        load(0, n - LAG).wait()
        project(0, n - LAG)
        hand_over(n - 2)

        @pl.when(jnp.logical_and(n > LAG, n < ROUNDS - 1))
        def _():
            project_late(n - LAG - 1, 0)

        return carry

    lax.fori_loop(LAG, ROUNDS, stage, 0)

    factor = math.log2(math.e) / math.sqrt(HEAD_SIZE)

    def target(step):
        return jnp.where(
            step == 3, s,
            jnp.where(step == 2, flipped(s, 1), jnp.where(step == 1, flipped(s, 3), flipped(s, 2))),
        )

    def out_copy(i, part, slot, row_from, place):
        row = 4 * jnp.where(i == 0, x, 1 - x) + row_from
        return remote(
            q_held.at[i, place, part], out.at[row, part], out_send.at[slot], out_recv.at[slot],
            {"seq": place, "adapt": a},
        )

    def own_out(i, part, slot):
        row = 4 * jnp.where(i == 0, x, 1 - x) + s
        return pltpu.make_async_copy(q_held.at[i, s, part], out.at[row, part], out_recv.at[slot])

    def placed(slot):
        far = slot < 8
        i = jnp.where(far, slot // 4, lax.rem(slot // 2, 2))
        step = jnp.where(far, lax.rem(slot // 2, 2), slot // 4)
        return i, step, lax.rem(slot, 2), target(step)

    def attend_step(slot, carry):
        i, step, part, place = placed(slot)

        @pl.when(slot == 2)
        def _():
            hand_over(ROUNDS - 2)
            hand_over(ROUNDS - 1)

        @pl.when(slot == 4)
        def _():
            lax.fori_loop(ROUNDS // 2 - 2, ROUNDS // 2, project_late, 0)

        for r in range(2):
            @pl.when(slot == 4 * r)
            def _():
                own_text(r).wait()
                for k in range(1, 4):
                    text_in(r, k).wait_recv()

        def scores(h):
            head = slice(h * HEAD_SIZE, (h + 1) * HEAD_SIZE)
            query = q_held[i, place, part, :, :, head].reshape(half_rows, HEAD_SIZE)
            image_keys = k_held[i, :, :, :, :, head].reshape(4 * token_local, HEAD_SIZE)
            text_keys = txt[i, :, :, head].reshape(text_rows, HEAD_SIZE)
            return tuple(
                lax.dot_general(
                    query, key_rows, (((1,), (1,)), ((), ())), preferred_element_type=F32
                )
                for key_rows in (image_keys, text_keys)
            )

        ready = scores(0)
        for h in range(heads):
            one, two = ready
            if h + 1 < heads:
                ready = scores(h + 1)
            head = slice(h * HEAD_SIZE, (h + 1) * HEAD_SIZE)
            value_head = slice(head_columns + h * HEAD_SIZE, head_columns + (h + 1) * HEAD_SIZE)
            highest = jnp.maximum(
                jnp.max(one, axis=-1, keepdims=True), jnp.max(two, axis=-1, keepdims=True)
            )
            one = jnp.exp2((one - highest) * factor)
            two = jnp.exp2((two - highest) * factor)
            share = 1.0 / (jnp.sum(one, axis=-1, keepdims=True) + jnp.sum(two, axis=-1, keepdims=True))
            image_values = v_held[i, :, :, :, :, head].reshape(4 * token_local, HEAD_SIZE)
            text_values = txt[i, :, :, value_head].reshape(text_rows, HEAD_SIZE)
            total = jnp.dot((one * share).astype(BF16), image_values, preferred_element_type=F32)
            total = total + jnp.dot(
                (two * share).astype(BF16), text_values, preferred_element_type=F32
            )
            q_held[i, place, part, :, :, head] = total.astype(BF16).reshape(
                ROUNDS, piece_rows, HEAD_SIZE
            )

        @pl.when(step == 3)
        def _():
            own_out(i, part, slot).start()

        @pl.when(step < 3)
        def _():
            out_copy(i, part, slot, s, place).start()

        return carry

    lax.fori_loop(0, 16, attend_step, 0)

    def finish_round(n, carry):
        end_round(n)
        for k in range(4):
            side(n, k).wait_send()
            across(n, k).wait_send()
            last(n, k).wait_send()
        return carry

    lax.fori_loop(0, ROUNDS, finish_round, 0)
    for copy in near_copies() + far_copies():
        copy.wait_send()
    for k in range(1, 4):
        spread_copy(k).wait_send()
        for i in range(2):
            text_copy(i, k).wait_send()

    def finish_out(slot, carry):
        i, step, part, place = placed(slot)

        @pl.when(step == 3)
        def _():
            own_out(i, part, slot).wait()

        @pl.when(step < 3)
        def _():
            out_copy(i, part, slot, place, place).wait()

        return carry

    lax.fori_loop(0, 16, finish_out, 0)


def on_device(
    image,
    modulation,
    query_key_value_weight,
    pooled_down_factor,
    pooled_up_factor,
    request_adapter,
    adapter_slot_table,
    row_request,
    text_key_value,
    query_key_gain,
):
    all_requests = request_adapter.shape[0]
    pool_local, width, rank = pooled_down_factor.shape
    columns = query_key_value_weight.shape[1]
    head_columns = columns // 3
    text_local = text_key_value.shape[1]
    token_local = image.shape[1]
    share = width // 4
    piece_rows = token_local // (2 * ROUNDS)
    held = pltpu.VMEM((2, 4, 2, ROUNDS, piece_rows, head_columns), BF16)

    def dma(*shape):
        return pltpu.SemaphoreType.DMA(shape)

    out, _ = pl.pallas_call(
        block_kernel,
        out_shape=(
            jax.ShapeDtypeStruct((all_requests, 2, ROUNDS, piece_rows, head_columns), BF16),
            jax.ShapeDtypeStruct((2, 4, 2, ROUNDS, piece_rows, width), BF16),
        ),
        in_specs=[ANY, WHOLE, ANY, ANY, ANY, WHOLE, ANY] + [SCALARS] * 3,
        out_specs=(ANY, ANY),
        scratch_shapes=[
            pltpu.VMEM((width, columns), BF16),
            pltpu.VMEM((2, 2, ROUNDS, piece_rows, width), BF16),
            pltpu.VMEM((2, 4, 2, 2, piece_rows, width), BF16),
            held, held, held,
            pltpu.VMEM((2, 4, text_local, 2 * head_columns), BF16),
            pltpu.VMEM((pool_local, rank, columns), BF16),
            pltpu.VMEM((pool_local, rank, share), BF16),
            pltpu.VMEM((2, 2, rank, columns), BF16),
            pltpu.VMEM((2, 2, rank, share), BF16),
            pltpu.VMEM((2, 2, rank, columns), BF16),
            pltpu.VMEM((2, 2, rank, share), BF16),
            pltpu.VMEM((2, rank, columns), BF16),
            pltpu.VMEM((2, rank, share), BF16),
            pltpu.VMEM((2, rank, columns), BF16),
            pltpu.VMEM((2, rank, share), BF16),
            pltpu.VMEM((4, 2, rank, share), BF16),
            pltpu.VMEM((2, rank, width), BF16),
            dma(ROUNDS), dma(), dma(2), dma(2),
        ]
        + [dma(ROUNDS, 4)] * 8
        + [dma(4)] * 2 + [dma(2)] * 2 + [dma(4)] * 2
        + [dma(2, 4)] * 2 + [dma(16)] * 2,
        compiler_params=pltpu.CompilerParams(
            collective_id=0, has_side_effects=True, vmem_limit_bytes=58 * 2**20
        ),
        name="block",
    )(
        image.reshape(2, 2, ROUNDS, piece_rows, width),
        modulation,
        query_key_value_weight,
        jnp.transpose(pooled_down_factor, (0, 2, 1)),
        pooled_up_factor,
        query_key_gain,
        text_key_value.reshape(2, 4, text_local, 2 * head_columns),
        request_adapter,
        adapter_slot_table,
        row_request,
    )
    return out.reshape(all_requests, token_local, head_columns)


def solution(mesh):
    in_specs = (
        P(("groups", "adapt"), "seq", None),
        P(("groups", "adapt"), None, None),
        P(None, "adapt"),
        P("seq", None, None),
        P("seq", None, "adapt"),
        P("groups"),
        P(),
        P("groups"),
        P("groups", "seq", None, "adapt"),
        P(),
    )
    out_specs = P("groups", "seq", "adapt")
    def chosen(*operands):
        image, request_adapter = operands[0], operands[5]
        fits = (
            mesh.shape["seq"] == 4
            and mesh.shape["adapt"] == 4
            and request_adapter.shape[0] == 8
            and image.shape[0] == 2
            and operands[2].shape[1] % (6 * HEAD_SIZE) == 0
            and image.shape[1] % 256 == 0
            and image.shape[2] % 512 == 0
        )
        return (on_device if fits else general_device)(*operands)

    return jax.shard_map(
        chosen, mesh=mesh, in_specs=in_specs, out_specs=out_specs, check_vma=False
    )
```
